256 devices in a mesh: tm: 32 (over z, y), space: 8 (over x, core).
Axes of the slice: x: 4, y: 4, z: 8, core: 2. Of those that a mesh axis runs over, the one named last changes fastest.
Arguments:
- density: bfloat16 [8192, 256, 128], P('tm', 'space'), may hold values from -6 to 6
- active: int32 [8192], P('tm'), may hold values from 1 to 256
- neighbours: int32 [256, 8], P('space'), may hold values from 0 to 255, as said below
- near_blocks: bfloat16 [2, 256, 8, 128, 128], P(None, 'space'), may hold values from -0.125 to 0.125
- to_moments: bfloat16 [64, 256, 128], P(None, 'space'), may hold values from -0.03125 to 0.03125
- from_moments: bfloat16 [64, 256, 128], P(None, 'space'), may hold values from -0.75 to 0.75
- decay_rates: float32 [64], replicated, may hold values from 2.4414063e-05 to 0.05, as said below
- lengths: float32 [8192], P('tm'), may hold values from 0.5 to 4096, as said below
Outputs:
- potential: bfloat16 [8192, 256, 128], P('tm', 'space')
The draws below stay inside these ranges and needn't reach their ends.
Inputs may be any that keep to these rules, and one draw needn't show every extreme that they name: `neighbours`: every entry of row c lies within 8 of c; each row names c - 8 and c + 8, clipped to the clusters that exist. `decay_rates`: positive rates. Positive lengths.
All inputs are finite; a program needn't handle non-finite values.
Results may differ from the reference program's by a relative error of at most 0.0085.
Values may be sent and summed in bfloat16 or wider, within the bound.
No kernel may reach another device: no remote copies, remote signals or barrier semaphores. Data moves between devices by JAX's collectives and lax.ppermute only.
A program may use at most 128 MiB of HBM per device.

```python
import jax
import jax.numpy as jnp
from jax import lax

ELEM = 128
TERMS = 64
NB = 8
REACH = 8
NT = 8192
NC = 256


def draw_neighbours(key, part):
    offsets = jax.random.randint(key, (NC, NB), -REACH, REACH + 1)
    scores = jax.random.randint(jax.random.fold_in(key, 3), (NC, NB), 0, 1 << 20) * NB + jnp.arange(NB, dtype=jnp.int32)[None, :]
    order = jnp.argsort(scores, axis=1)
    ranks = jnp.argsort(order, axis=1)
    offsets = jnp.where(ranks == 0, REACH, jnp.where(ranks == 1, -REACH, offsets))
    result = jnp.clip(jnp.arange(NC, dtype=jnp.int32)[:, None] + offsets, 0, NC - 1)
    return result.astype(jnp.int32)


def draw_decay_rates(key, part):
    pick = jax.random.uniform(jax.random.fold_in(key, 11), (TERMS,))
    share = 0.5
    slow_log = jax.random.uniform(jax.random.fold_in(key, 12), (TERMS,), minval=jnp.log(0.2 / NT), maxval=jnp.log(0.8 / NT))
    fast_log = jax.random.uniform(jax.random.fold_in(key, 13), (TERMS,), minval=jnp.log(0.02), maxval=jnp.log(0.05))
    return jnp.where(pick < share, jnp.exp(slow_log), jnp.exp(fast_log)).astype(jnp.float32)


def draw_lengths(key, part):
    base = jax.random.uniform(key, (NT,), minval=0.5, maxval=2.0)
    places = jax.random.randint(jax.random.fold_in(key, 5), (3,), 0, NT)
    base = base.at[places].set(jnp.float32(NT // 2))
    return base.astype(jnp.float32)


def touch_ends(values, stream_key, low, high):
    spot = [jax.random.randint(jax.random.fold_in(stream_key, axis), (), 0, length) for axis, length in enumerate(values.shape)]
    longest = values.shape.index(max(values.shape))
    neighbour = spot[:longest] + [(spot[longest] + 1) % values.shape[longest]] + spot[longest + 1:]
    return values.at[tuple(spot)].set(low).at[tuple(neighbour)].set(high)


def levels(stream_key, dims, split, low, largest):
    loudness = 1.0
    for axis_at, parts in split:
        steps = jax.random.uniform(jax.random.fold_in(jax.random.fold_in(stream_key, 6), axis_at), (parts,), jnp.float32, low / len(split), largest / len(split))
        loudness = loudness * jnp.repeat(jnp.exp(steps), dims[axis_at] // parts).reshape((-1,) + (1,) * (len(dims) - 1 - axis_at))
    return loudness


def bell_draw(own_key, dims, deviation, bound, split=(), kind=jnp.bfloat16):
    factor_of = levels(own_key, dims, split, -0.22, 0.18) if split else 1.0
    values = jax.random.normal(own_key, dims, jnp.float32) * deviation * factor_of
    return jnp.minimum(jnp.maximum(values, -bound), bound).astype(kind)


def setup_inputs(seed: int = 0) -> dict:
    key_list = jax.random.split(jax.random.key(seed), 9)
    return {
        "density": bell_draw(key_list[0], (NT, NC, ELEM), 1.0, 6.0, ((0, 32), (1, 8))),
        "active": touch_ends(jax.random.randint(key_list[1], (NT,), 1, NC + 1), jax.random.fold_in(key_list[1], 1), 1, NC).astype(jnp.int32),
        "neighbours": draw_neighbours(jax.random.fold_in(key_list[8], 71), 0),
        "near_blocks": bell_draw(key_list[3], (2, NC, NB, ELEM, ELEM), (2 * NB * ELEM) ** -0.5, 0.125, ((1, 8),)),
        "to_moments": bell_draw(key_list[4], (TERMS, NC, ELEM), (NC * ELEM) ** -0.5, 0.03125, ((1, 8),)),
        "from_moments": bell_draw(key_list[5], (TERMS, NC, ELEM), TERMS ** -0.5, 0.75, ((1, 8),)),
        "decay_rates": draw_decay_rates(jax.random.fold_in(key_list[8], 71), 0),
        "lengths": draw_lengths(jax.random.fold_in(key_list[8], 71), 0),
    }


def reference(density, active, neighbours, near_blocks, to_moments, from_moments, decay_rates, lengths):
    live_mask = (jnp.arange(NC, dtype=jnp.int32)[None, :] < active[:, None]).astype(jnp.bfloat16)
    masked = density * live_mask[:, :, None]
    earlier = jnp.concatenate([jnp.zeros((1, NC, ELEM), jnp.bfloat16), masked[:-1]], 0)

    def one_cluster(cluster):
        chosen = neighbours[cluster]
        current = jnp.take(masked, chosen, axis=1).astype(jnp.float32)
        previous = jnp.take(earlier, chosen, axis=1).astype(jnp.float32)
        blocks = near_blocks[:, cluster].astype(jnp.float32)
        return jnp.einsum('tje,jef->tf', current, blocks[0]) + jnp.einsum('tje,jef->tf', previous, blocks[1])
    near_term = lax.map(one_cluster, jnp.arange(NC, dtype=jnp.int32))
    near_term = jnp.transpose(near_term, (1, 0, 2))
    flat = masked.reshape(NT, NC * ELEM)
    moments = jnp.dot(flat, to_moments.reshape(TERMS, NC * ELEM).T, preferred_element_type=jnp.float32)
    decays = jnp.exp(-decay_rates[None, :] * lengths[:, None])

    def advance(state, inputs):
        factor, moment = inputs
        return (factor * state + moment, state)
    _, far_coeff = lax.scan(advance, jnp.zeros((TERMS,), jnp.float32), (decays, moments))
    scaled = (far_coeff * jnp.sqrt(2.0 * decay_rates)[None, :]).astype(jnp.bfloat16)
    far_term = jnp.dot(scaled, from_moments.reshape(TERMS, NC * ELEM), preferred_element_type=jnp.float32)
    far_term = far_term.reshape(NT, NC, ELEM)
    return (live_mask.astype(jnp.float32)[:, :, None] * (near_term + far_term)).astype(jnp.bfloat16)
```

```python
import functools

import jax
import jax.numpy as jnp
from jax import lax
from jax.experimental import pallas as pl
from jax.experimental.pallas import tpu as pltpu
from jax.sharding import PartitionSpec as P

REACH = 8
F32 = jnp.float32
BF16 = jnp.bfloat16


def column(row, lanes):
    return jnp.transpose(jnp.broadcast_to(row, (lanes, row.shape[1])))


def shifted_down(v, steps, fill):
    rows = v.shape[0]
    if steps < 8:
        moved = pltpu.roll(v, steps, 0)
        at = lax.broadcasted_iota(jnp.int32, v.shape, 0)
        return jnp.where(at < steps, jnp.full_like(v, fill), moved)
    return jnp.concatenate([jnp.full((steps, v.shape[1]), fill, v.dtype), v[: rows - steps]], 0)


def doubled(row):
    return jnp.concatenate([row, row], axis=1)


def prep_kernel(
    steps,
    density,
    active,
    to_moments,
    rates,
    lengths,
    low,
    mid,
    high,
    far,
    decay,
    ends,
    flat,
    flat_map,
    live,
):
    step = pl.program_id(0)
    last = pl.num_programs(0) - 1
    chunk, clusters, unknowns = density.shape
    terms = to_moments.shape[0]
    first = lax.axis_index("space") * clusters

    @pl.when(step == 0)
    def _():
        live[...] = column(active[...], unknowns)

    flat[...] = density[...].astype(F32).reshape(chunk * clusters, unknowns)
    here = pl.ds(pl.multiple_of(step * chunk, chunk), chunk)
    alive = live[here, :]

    def place(c):
        if c < REACH:
            return low, c
        if c < clusters - REACH:
            return mid, c - REACH
        return high, c - (clusters - REACH)

    for c in range(clusters):
        x = flat[pl.ds(c, chunk, stride=clusters), :]
        x = jnp.where(alive > first + c, x, 0.0).astype(BF16)
        ref, at = place(c)
        ref[at, here, :] = x

    @pl.when(step == last)
    def _():
        flat_map[...] = to_moments[...].astype(F32).reshape(terms * clusters, unknowns)
        total = jnp.zeros((steps, 2 * terms), F32)
        for c in range(0, clusters, 2):
            a, i = place(c)
            b, j = place(c + 1)
            x = jnp.concatenate([a[i], b[j]], axis=1)
            w = jnp.concatenate(
                [
                    flat_map[pl.ds(c, terms, stride=clusters), :].astype(BF16),
                    flat_map[pl.ds(c + 1, terms, stride=clusters), :].astype(BF16),
                ],
                axis=1,
            )
            w = jnp.concatenate([w, w], axis=0)
            total = total + lax.dot_general(
                x, w, (((1,), (1,)), ((), ())), preferred_element_type=F32
            )
        d = jnp.exp(-doubled(rates[...]) * column(lengths[...], 2 * terms))
        s = 1
        while s < steps:
            before = shifted_down(total, s, 0.0)
            factor = shifted_down(d, s, 1.0)
            total = total + d * before
            d = d * factor
            s *= 2
        far[...] = shifted_down(total, 1, 0.0)
        decay[...] = shifted_down(d, 1, 1.0)
        lane = lax.broadcasted_iota(jnp.int32, (1, 2 * terms), 1)
        line = jnp.where(lane < terms, total[steps - 1 :], d[steps - 1 :])
        for k in range(ends.shape[0]):
            ends[k] = line


def prep(density, active, to_moments, rates, lengths, slabs):
    steps, clusters, unknowns = density.shape
    terms = to_moments.shape[0]
    chunk = 64
    whole = lambda *shape: pl.BlockSpec(shape, lambda i: (0,) * len(shape))

    return pl.pallas_call(
        functools.partial(prep_kernel, steps),
        grid=(steps // chunk,),
        in_specs=[
            pl.BlockSpec((chunk, clusters, unknowns), lambda i: (i, 0, 0)),
            whole(1, steps),
            whole(terms, clusters, unknowns),
            whole(1, terms),
            whole(1, steps),
        ],
        out_specs=[
            whole(REACH, steps, unknowns),
            whole(clusters - 2 * REACH, steps, unknowns),
            whole(REACH, steps, unknowns),
            whole(steps, 2 * terms),
            whole(steps, 2 * terms),
            whole(slabs, 1, 2 * terms),
        ],
        out_shape=[
            jax.ShapeDtypeStruct((REACH, steps, unknowns), BF16),
            jax.ShapeDtypeStruct((clusters - 2 * REACH, steps, unknowns), BF16),
            jax.ShapeDtypeStruct((REACH, steps, unknowns), BF16),
            jax.ShapeDtypeStruct((steps, 2 * terms), F32),
            jax.ShapeDtypeStruct((steps, 2 * terms), F32),
            jax.ShapeDtypeStruct((slabs, 1, 2 * terms), F32),
        ],
        scratch_shapes=[
            pltpu.VMEM((chunk * clusters, unknowns), F32),
            pltpu.VMEM((terms * clusters, unknowns), F32),
            pltpu.VMEM((steps, unknowns), jnp.int32),
        ],
        compiler_params=pltpu.CompilerParams(vmem_limit_bytes=24 << 20),
        name="prep",
    )(density, active, to_moments, rates, lengths)


def arrive_kernel(ends, far, decay, out):
    me = lax.axis_index("tm")
    slabs = ends.shape[0]
    steps, lanes = far.shape
    half = lanes // 2
    lane = lax.broadcasted_iota(jnp.int32, (1, lanes), 1)
    state = jnp.zeros((1, lanes), F32)
    for k in range(slabs):
        v = ends[k]
        other = pltpu.roll(v, half, 1)
        end = jnp.where(lane < half, v, other)
        factor = jnp.where(lane < half, other, v)
        state = jnp.where(k < me, factor * state + end, state)
    x = far[...] + decay[...] * state
    wide = lax.broadcasted_iota(jnp.int32, (steps // 2, lanes), 1)
    packed = jnp.where(wide < half, x[: steps // 2], x[steps // 2 :]).astype(BF16)
    for k in range(out.shape[0]):
        out[k] = packed


def arrive(ends, far, decay, peers):
    steps, lanes = far.shape
    return pl.pallas_call(
        arrive_kernel,
        out_shape=jax.ShapeDtypeStruct((peers, steps // 2, lanes), BF16),
        name="arrive",
    )(ends, far, decay)


def near_kernel(offset, split, group, neighbours, *refs):
    sources = refs[: len(offset)]
    blocks, near, carry, window, sems = refs[len(offset) :]
    step = pl.program_id(0)

    @pl.when(step == 0)
    def _():
        copies = [
            pltpu.make_async_copy(src, window.at[pl.ds(at, src.shape[0])], sems.at[k])
            for k, (src, at) in enumerate(zip(sources, offset))
        ]
        for copy in copies:
            copy.start()
        for copy in copies:
            copy.wait()

    lags, _, nb, unknowns, _ = blocks.shape
    clusters = neighbours.shape[0]
    base = lax.axis_index("space") * clusters - REACH
    for g in range(group):
        here = step * group + g
        cluster = split(here)
        x = jnp.concatenate(
            [window[neighbours[cluster, j] - base] for j in range(nb)], axis=1
        )
        w = jnp.concatenate(
            [blocks[lag, g].reshape(nb * unknowns, unknowns) for lag in range(lags)], axis=1
        )
        both = jnp.dot(x, w, preferred_element_type=F32)
        now, later = both[:, :unknowns], both[:, unknowns:]
        near[g] = now + shifted_down(later, 1, 0.0)
        carry[g] = later[later.shape[0] - 1 :]


def near_field(neighbours, sources, offset, blocks, split, block_of, count, group):
    steps, unknowns = sources[0].shape[1:]
    lags, clusters, nb = blocks.shape[:3]

    return pl.pallas_call(
        functools.partial(near_kernel, offset, split, group),
        grid_spec=pltpu.PrefetchScalarGridSpec(
            num_scalar_prefetch=1,
            grid=(count // group,),
            in_specs=[pl.BlockSpec(memory_space=pl.ANY)] * len(sources)
            + [
                pl.BlockSpec(
                    (lags, group, nb, unknowns, unknowns),
                    lambda i, _: (0, block_of(i), 0, 0, 0),
                )
            ],
            out_specs=[
                pl.BlockSpec((group, steps, unknowns), lambda i, _: (i, 0, 0)),
                pl.BlockSpec((group, 1, unknowns), lambda i, _: (i, 0, 0)),
            ],
            scratch_shapes=[
                pltpu.VMEM((clusters + 2 * REACH, steps, unknowns), BF16),
                pltpu.SemaphoreType.DMA((len(sources),)),
            ],
        ),
        out_shape=[
            jax.ShapeDtypeStruct((count, steps, unknowns), F32),
            jax.ShapeDtypeStruct((count, 1, unknowns), F32),
        ],
        compiler_params=pltpu.CompilerParams(vmem_limit_bytes=24 << 20),
        name="near",
    )(neighbours, *sources, blocks)


def final_kernel(
    inner,
    outer,
    carry_in,
    carry_out,
    parts,
    from_moments,
    rates,
    active,
    out,
    flat,
    live,
    flat_map,
    maps,
    scaled,
):
    step = pl.program_id(0)
    chunk, clusters, unknowns = out.shape
    terms = from_moments.shape[0]
    steps = active.shape[1]
    first = lax.axis_index("space") * clusters

    @pl.when(step == 0)
    def _():
        live[...] = column(active[...], unknowns)
        flat_map[...] = from_moments[...].astype(F32).reshape(terms * clusters, unknowns)
        for c in range(clusters):
            w = flat_map[pl.ds(c, terms, stride=clusters), :].astype(BF16)
            maps[c // 2, :, pl.ds((c % 2) * unknowns, unknowns)] = jnp.concatenate([w, w], axis=0)
        total = parts[0].astype(F32)
        for k in range(1, parts.shape[0]):
            total = total + parts[k].astype(F32)
        scaled[...] = total * jnp.sqrt(2.0 * doubled(rates[...]))

    here = pl.ds(pl.multiple_of(step * chunk, chunk), chunk)
    alive = live[here, :]
    per_half = steps // 2 // chunk
    half = step // per_half
    mine = scaled[pl.ds(pl.multiple_of(lax.rem(step, per_half) * chunk, chunk), chunk), :]
    lane = lax.broadcasted_iota(jnp.int32, mine.shape, 1)
    mine = jnp.where(lane // terms == half, mine, 0.0).astype(BF16)
    row = lax.broadcasted_iota(jnp.int32, (chunk, unknowns), 0)
    starts = jnp.logical_and(row == 0, step == 0)
    for p in range(clusters // 2):
        both = jnp.dot(mine, maps[p], preferred_element_type=F32)
        for q in range(2):
            c = 2 * p + q
            if c < REACH:
                near, at, carry = outer, c, carry_out
            elif c < clusters - REACH:
                near, at, carry = inner, c - REACH, carry_in
            else:
                near, at, carry = outer, c - (clusters - 2 * REACH), carry_out
            x = both[:, q * unknowns : (q + 1) * unknowns] + near[at]
            x = x + jnp.where(starts, jnp.broadcast_to(carry[at], x.shape), 0.0)
            x = jnp.where(alive > first + c, x, 0.0)
            flat[pl.ds(c, chunk, stride=clusters), :] = x
    out[...] = flat[...].reshape(chunk, clusters, unknowns).astype(BF16)


def final(inner, outer, carry_in, carry_out, parts, from_moments, rates, active):
    count, steps, unknowns = inner.shape
    terms, clusters = from_moments.shape[:2]
    chunk = 64
    whole = lambda *shape: pl.BlockSpec(shape, lambda i: (0,) * len(shape))
    return pl.pallas_call(
        final_kernel,
        grid=(steps // chunk,),
        in_specs=[
            pl.BlockSpec((count, chunk, unknowns), lambda i: (0, i, 0)),
            pl.BlockSpec((outer.shape[0], chunk, unknowns), lambda i: (0, i, 0)),
            whole(*carry_in.shape),
            whole(*carry_out.shape),
            whole(*parts.shape),
            whole(*from_moments.shape),
            whole(1, terms),
            whole(1, steps),
        ],
        out_specs=pl.BlockSpec((chunk, clusters, unknowns), lambda i: (i, 0, 0)),
        out_shape=jax.ShapeDtypeStruct((steps, clusters, unknowns), BF16),
        scratch_shapes=[
            pltpu.VMEM((chunk * clusters, unknowns), F32),
            pltpu.VMEM((steps, unknowns), jnp.int32),
            pltpu.VMEM((terms * clusters, unknowns), F32),
            pltpu.VMEM((clusters // 2, 2 * terms, 2 * unknowns), BF16),
            pltpu.VMEM((steps // 2, 2 * terms), F32),
        ],
        compiler_params=pltpu.CompilerParams(vmem_limit_bytes=24 << 20),
        name="final",
    )(inner, outer, carry_in, carry_out, parts, from_moments, rates, active)


def exchanged(x, axis):
    return lax.all_to_all(x, axis, split_axis=0, concat_axis=0, tiled=True)


def passed_on(x, axis, distance):
    count = lax.axis_size(axis)
    route = [(i, i + distance) for i in range(count) if 0 <= i + distance < count]
    return lax.ppermute(x, axis, route)


def local(density, active, neighbours, near_blocks, to_moments, from_moments, decay_rates, lengths):
    steps, clusters, unknowns = density.shape
    slabs, peers = lax.axis_size("tm"), lax.axis_size("space")
    active = active.reshape(1, steps)
    lengths = lengths.reshape(1, steps)
    rates = decay_rates.reshape(1, -1)
    low, mid, high, far, decay, ends = prep(density, active, to_moments, rates, lengths, slabs)
    ends = exchanged(ends, "tm")
    from_below = passed_on(high, "space", 1)
    from_above = passed_on(low, "space", -1)
    inner_count = clusters - 2 * REACH
    group = 2
    inner, carry_in = near_field(
        neighbours,
        (low, mid, high),
        (REACH, 2 * REACH, clusters),
        near_blocks,
        lambda i: i + REACH,
        lambda i: i + REACH // group,
        inner_count,
        group,
    )
    parts = exchanged(arrive(ends, far, decay, peers), "space")
    half = REACH // group
    outer, carry_out = near_field(
        neighbours,
        (from_below, low, mid, high, from_above),
        (0, REACH, 2 * REACH, clusters, clusters + REACH),
        near_blocks,
        lambda i: jnp.where(i < REACH, i, i + inner_count),
        lambda i: jnp.where(i < half, i, i + inner_count // group),
        2 * REACH,
        group,
    )
    carry = passed_on(jnp.concatenate([carry_in, carry_out], axis=0), "tm", 1)
    return final(
        inner,
        outer,
        carry[:inner_count],
        carry[inner_count:],
        parts,
        from_moments,
        rates,
        active,
    )


def solution(mesh):
    placed = (
        P("tm", "space", None),
        P("tm"),
        P("space", None),
        P(None, "space", None, None, None),
        P(None, "space", None),
        P(None, "space", None),
        P(),
        P("tm"),
    )
    return jax.shard_map(
        local, mesh=mesh, in_specs=placed, out_specs=P("tm", "space", None), check_vma=False
    )
```

```python
import functools

import jax
import jax.numpy as jnp
from jax import lax
from jax.experimental import pallas as pl
from jax.experimental.pallas import tpu as pltpu
from jax.sharding import PartitionSpec as P

REACH = 8
F32 = jnp.float32
BF16 = jnp.bfloat16
HBM = pl.BlockSpec(memory_space=pltpu.HBM)
VMEM = pl.BlockSpec(memory_space=pltpu.VMEM)
SMEM = pl.BlockSpec(memory_space=pltpu.SMEM)


def in_hbm(x):
    return pltpu.with_memory_space_constraint(x, pltpu.HBM)


def in_vmem(x):
    return pltpu.with_memory_space_constraint(x, pltpu.VMEM)


def column(row, lanes):
    return jnp.transpose(jnp.broadcast_to(row, (lanes, row.shape[1])))


def shifted_down(v, steps, fill):
    rows = v.shape[0]
    if steps < 8:
        moved = pltpu.roll(v, steps, 0)
        at = lax.broadcasted_iota(jnp.int32, v.shape, 0)
        return jnp.where(at < steps, jnp.full_like(v, fill), moved)
    return jnp.concatenate([jnp.full((steps, v.shape[1]), fill, v.dtype), v[: rows - steps]], 0)


def doubled(row):
    return jnp.concatenate([row, row], axis=1)


def is_even():
    return lax.rem(lax.axis_index("space"), 2) == 0


def prep_kernel(
    density,
    active,
    to_moments,
    rates,
    lengths,
    window,
    pair,
    other,
    far,
    decay,
    ends,
    live,
    dense,
    maps,
    active_row,
    rates_row,
    lengths_row,
    flat,
    sems,
):
    steps, clusters, unknowns = density.shape
    terms = to_moments.shape[0]
    pieces = 4
    size = steps // pieces
    chunk = 32
    pitch = clusters + 1
    first = lax.axis_index("space") * clusters

    def copy(src, dst, k):
        return pltpu.make_async_copy(src, dst, sems.at[k])

    small = [
        copy(active, active_row, 0),
        copy(lengths, lengths_row, 1),
        copy(rates, rates_row, 2),
    ]
    parts = [
        copy(density.at[pl.ds(k * size, size)], dense.at[pl.ds(k * size, size)], 4 + k)
        for k in range(pieces)
    ]
    weights = copy(to_moments, maps, 3)
    for c in small + parts + [weights]:
        c.start()
    for c in small:
        c.wait()
    live[...] = column(active_row[...], unknowns)

    for k in range(pieces):
        parts[k].wait()

        def spread(i, _):
            start = pl.multiple_of(k * size + i * chunk, chunk)
            here = pl.ds(start, chunk)
            x = dense[here].astype(F32)
            for t in range(chunk):
                flat[pl.ds(t * pitch, clusters), :] = x[t]
            alive = live[here, :]
            for c in range(clusters):
                y = flat[pl.ds(c, chunk, stride=pitch), :]
                y = jnp.where(alive > first + c, y, 0.0)
                window[REACH + c, here, :] = y.astype(BF16)
            return 0

        lax.fori_loop(0, size // chunk, spread, 0)

    even = is_even()
    above = clusters
    sides = [
        copy(window.at[pl.ds(jnp.where(even, above, REACH), REACH)], pair, 8),
        copy(window.at[pl.ds(jnp.where(even, REACH, above), REACH)], other, 9),
    ]
    for c in sides:
        c.start()

    weights.wait()
    w = jnp.transpose(maps[...], (1, 0, 2))
    total = jnp.zeros((steps, 2 * terms), F32)
    for c in range(0, clusters, 2):
        x = jnp.concatenate([window[REACH + c], window[REACH + c + 1]], axis=1)
        y = jnp.concatenate([w[c], w[c + 1]], axis=1)
        y = jnp.concatenate([y, y], axis=0)
        total = total + lax.dot_general(
            x, y, (((1,), (1,)), ((), ())), preferred_element_type=F32
        )
    d = jnp.exp(-doubled(rates_row[...]) * column(lengths_row[...], 2 * terms))
    s = 1
    while s < steps:
        before = shifted_down(total, s, 0.0)
        factor = shifted_down(d, s, 1.0)
        total = total + d * before
        d = d * factor
        s *= 2
    lane = lax.broadcasted_iota(jnp.int32, (1, 2 * terms), 1)
    line = jnp.where(lane < terms, total[steps - 1 :], d[steps - 1 :])
    for k in range(ends.shape[0]):
        ends[k] = line
    scale = jnp.sqrt(2.0 * doubled(rates_row[...]))
    far[...] = shifted_down(total, 1, 0.0) * scale
    decay[...] = shifted_down(d, 1, 1.0) * scale
    for c in sides:
        c.wait()


def prep(density, active, to_moments, rates, lengths, slabs):
    steps, clusters, unknowns = density.shape
    terms = to_moments.shape[0]
    lanes = 2 * terms
    side = pltpu.HBM((REACH, steps, unknowns), BF16)
    return pl.pallas_call(
        prep_kernel,
        in_specs=[HBM] * 5,
        out_specs=[VMEM, HBM, HBM] + [VMEM] * 4,
        out_shape=[
            jax.ShapeDtypeStruct((clusters + 2 * REACH, steps, unknowns), BF16),
            side,
            side,
            jax.ShapeDtypeStruct((steps, lanes), F32),
            jax.ShapeDtypeStruct((steps, lanes), F32),
            jax.ShapeDtypeStruct((slabs, 1, lanes), F32),
            jax.ShapeDtypeStruct((steps, unknowns), jnp.int32),
        ],
        scratch_shapes=[
            pltpu.VMEM(density.shape, BF16),
            pltpu.VMEM(to_moments.shape, BF16),
            pltpu.VMEM(active.shape, jnp.int32),
            pltpu.VMEM(rates.shape, F32),
            pltpu.VMEM(lengths.shape, F32),
            pltpu.VMEM((32 * (clusters + 1) + 7, unknowns), F32),
            pltpu.SemaphoreType.DMA((10,)),
        ],
        compiler_params=pltpu.CompilerParams(vmem_limit_bytes=10 << 20),
        name="prep",
    )(*map(in_hbm, (density, active, to_moments, rates, lengths)))


def arrive_kernel(ends, far, decay, out):
    me = lax.axis_index("tm")
    slabs = ends.shape[0]
    steps, lanes = far.shape
    half = lanes // 2
    lane = lax.broadcasted_iota(jnp.int32, (1, lanes), 1)
    state = jnp.zeros((1, lanes), F32)
    for k in range(slabs):
        v = ends[k]
        swapped = pltpu.roll(v, half, 1)
        end = jnp.where(lane < half, v, swapped)
        factor = jnp.where(lane < half, swapped, v)
        state = jnp.where(k < me, factor * state + end, state)
    x = far[...] + decay[...] * state
    wide = lax.broadcasted_iota(jnp.int32, (steps // 2, lanes), 1)
    out[...] = jnp.where(wide < half, x[: steps // 2], x[steps // 2 :])


def arrive(ends, far, decay):
    steps, lanes = far.shape
    return pl.pallas_call(
        arrive_kernel,
        in_specs=[VMEM] * 3,
        out_specs=VMEM,
        out_shape=jax.ShapeDtypeStruct((steps // 2, lanes), F32),
        compiler_params=pltpu.CompilerParams(vmem_limit_bytes=4 << 20),
        name="arrive",
    )(ends, far, decay)


def pair_kernel(a, b, out):
    out[...] = (a[...] + b[...]).astype(BF16)


def pair_sum(a, b):
    return pl.pallas_call(
        pair_kernel,
        in_specs=[VMEM] * 2,
        out_specs=VMEM,
        out_shape=jax.ShapeDtypeStruct(a.shape, BF16),
        compiler_params=pltpu.CompilerParams(vmem_limit_bytes=4 << 20),
        name="pair_sum",
    )(a, b)


def near_fetches(blocks, held, sems, order):
    return [
        [
            pltpu.make_async_copy(blocks.at[lag, c], held.at[lag, i], sems.at[lag, i])
            for lag in range(blocks.shape[0])
        ]
        for i, c in enumerate(order)
    ]


def near_of(neighbours, window, held, fetches, i, cluster):
    lags, _, nb, unknowns, _ = held.shape
    base = lax.axis_index("space") * neighbours.shape[1] - REACH
    for fetch in fetches[i]:
        fetch.wait()
    x = jnp.concatenate([window[neighbours[j, cluster] - base] for j in range(nb)], axis=1)
    w = jnp.concatenate(
        [held[lag, i].reshape(nb * unknowns, unknowns) for lag in range(lags)], axis=1
    )
    both = jnp.dot(x, w, preferred_element_type=F32)
    now, later = both[:, :unknowns], both[:, unknowns:]
    last = pltpu.roll(later[later.shape[0] - 8 :], 1, 0)
    return now + shifted_down(later, 1, 0.0), last


def inner_kernel(order, neighbours, window, blocks, near, held, found, sems, out_sems):
    steps = window.shape[1]
    fetches = near_fetches(blocks, held, sems, order)
    for some in fetches:
        for fetch in some:
            fetch.start()
    stores = []
    for i, cluster in enumerate(order):
        x, last = near_of(neighbours, window, held, fetches, i, cluster)
        found[i, :steps, :] = x
        found[i, steps:, :] = last
        stores.append(pltpu.make_async_copy(found.at[i], near.at[i], out_sems.at[i]))
        stores[-1].start()
    for store in stores:
        store.wait()


def inner_near(neighbours, window, blocks):
    steps, unknowns = window.shape[1:]
    lags, clusters, nb = blocks.shape[:3]
    order = tuple(range(REACH, clusters - REACH))
    count = len(order)
    return pl.pallas_call(
        functools.partial(inner_kernel, order),
        in_specs=[SMEM, VMEM, HBM],
        out_specs=HBM,
        out_shape=pltpu.HBM((count, steps + 8, unknowns), F32),
        scratch_shapes=[
            pltpu.VMEM((lags, count, nb, unknowns, unknowns), BF16),
            pltpu.VMEM((count, steps + 8, unknowns), F32),
            pltpu.SemaphoreType.DMA((lags, count)),
            pltpu.SemaphoreType.DMA((count,)),
        ],
        compiler_params=pltpu.CompilerParams(vmem_limit_bytes=16 << 20),
        name="inner",
    )(neighbours, window, in_hbm(blocks))


def outer_kernel(
    order,
    neighbours,
    window_in,
    from_pair,
    from_other,
    blocks,
    inner,
    from_moments,
    near,
    carry,
    maps,
    window,
    held,
    rows,
    sems,
    side_sems,
):
    del window_in
    steps = window.shape[1]
    even = is_even()
    above = window.shape[0] - REACH

    def copy(src, dst, k):
        return pltpu.make_async_copy(src, dst, side_sems.at[k])

    sides = [
        copy(from_pair, window.at[pl.ds(jnp.where(even, above, 0), REACH)], 0),
        copy(from_other, window.at[pl.ds(jnp.where(even, 0, above), REACH)], 1),
    ]
    inner_copy = copy(inner, near.at[pl.ds(REACH, inner.shape[0])], 2)
    rows_copy = copy(from_moments, rows, 3)
    fetches = near_fetches(blocks, held, sems, order)
    for c in sides:
        c.start()
    for some in fetches:
        for fetch in some:
            fetch.start()
    inner_copy.start()
    rows_copy.start()
    for c in sides:
        c.wait()
    for i, cluster in enumerate(order):
        x, last = near_of(neighbours, window, held, fetches, i, cluster)
        near[cluster, :steps, :] = x
        carry[cluster] = last[:1]
    inner_copy.wait()
    for i in range(inner.shape[0]):
        carry[REACH + i] = near[REACH + i, steps : steps + 1, :]
    rows_copy.wait()
    w = jnp.transpose(rows[...], (1, 0, 2))
    for p in range(maps.shape[0]):
        x = jnp.concatenate([w[2 * p], w[2 * p + 1]], axis=1)
        maps[p] = jnp.concatenate([x, x], axis=0)


def outer_near(neighbours, window, from_pair, from_other, blocks, inner, from_moments):
    steps, unknowns = window.shape[1:]
    lags, clusters, nb = blocks.shape[:3]
    terms = from_moments.shape[0]
    order = tuple(range(REACH)) + tuple(range(clusters - REACH, clusters))
    count = len(order)
    return pl.pallas_call(
        functools.partial(outer_kernel, order),
        in_specs=[SMEM, VMEM] + [HBM] * 5,
        out_specs=[VMEM] * 4,
        out_shape=[
            jax.ShapeDtypeStruct((clusters, steps + 8, unknowns), F32),
            jax.ShapeDtypeStruct((clusters, 1, unknowns), F32),
            jax.ShapeDtypeStruct((clusters // 2, 2 * terms, 2 * unknowns), BF16),
            jax.ShapeDtypeStruct(window.shape, BF16),
        ],
        scratch_shapes=[
            pltpu.VMEM((lags, count, nb, unknowns, unknowns), BF16),
            pltpu.VMEM(from_moments.shape, BF16),
            pltpu.SemaphoreType.DMA((lags, count)),
            pltpu.SemaphoreType.DMA((4,)),
        ],
        input_output_aliases={1: 3},
        compiler_params=pltpu.CompilerParams(vmem_limit_bytes=14 << 20),
        name="outer",
    )(
        neighbours,
        window,
        in_hbm(from_pair),
        in_hbm(from_other),
        in_hbm(blocks),
        in_hbm(inner),
        in_hbm(from_moments),
    )


def final_kernel(near, carry, *refs):
    parts = refs[:4]
    maps, live, out, major, done, sems = refs[4:]
    steps, clusters, unknowns = out.shape
    terms = maps.shape[1] // 2
    first = lax.axis_index("space") * clusters
    total = parts[0][...].astype(F32)
    for part in parts[1:]:
        total = total + part[...].astype(F32)
    lane = lax.broadcasted_iota(jnp.int32, total.shape, 1)
    size = steps // 2
    chunk = 32
    row = lax.broadcasted_iota(jnp.int32, (8, unknowns), 0)
    copies = []
    for half in range(2):
        mine = jnp.where(lane // terms == half, total, 0.0).astype(BF16)
        here = pl.ds(half * size, size)
        alive = live[here, :]
        for p in range(clusters // 2):
            both = jnp.dot(mine, maps[p], preferred_element_type=F32)
            for q in range(2):
                c = 2 * p + q
                x = both[:, q * unknowns : (q + 1) * unknowns] + near[c, here, :]
                if half == 0:
                    head = jnp.where(row == 0, jnp.broadcast_to(carry[c], row.shape), 0.0)
                    x = jnp.concatenate([x[:8] + head, x[8:]], axis=0)
                major[c] = jnp.where(alive > first + c, x, 0.0).astype(BF16)
        for i in range(size // chunk):
            at = half * size + i * chunk
            done[pl.ds(at, chunk)] = jnp.transpose(major[:, pl.ds(i * chunk, chunk), :], (1, 0, 2))
            copies.append(
                pltpu.make_async_copy(
                    done.at[pl.ds(at, chunk)], out.at[pl.ds(at, chunk)], sems.at[at // chunk]
                )
            )
            copies[-1].start()
    for copy in copies:
        copy.wait()


def final(near, carry, parts, maps, live):
    steps, unknowns = live.shape
    clusters = near.shape[0]
    return pl.pallas_call(
        final_kernel,
        in_specs=[VMEM] * (4 + len(parts)),
        out_specs=HBM,
        out_shape=jax.ShapeDtypeStruct((steps, clusters, unknowns), BF16),
        scratch_shapes=[
            pltpu.VMEM((clusters, steps // 2, unknowns), BF16),
            pltpu.VMEM((steps, clusters, unknowns), BF16),
            pltpu.SemaphoreType.DMA((steps // 32,)),
        ],
        compiler_params=pltpu.CompilerParams(vmem_limit_bytes=10 << 20),
        name="final",
    )(near, carry, *parts, maps, live)


def exchanged(x, axis):
    return lax.all_to_all(x, axis, split_axis=0, concat_axis=0, tiled=True)


def swapped_from(x, axis, start):
    count = lax.axis_size(axis)
    route = []
    for i in range(start, count - 1, 2):
        route += [(i, i + 1), (i + 1, i)]
    return lax.ppermute(x, axis, route)


def from_chip(x, axis, distance):
    count = lax.axis_size(axis)
    return lax.ppermute(x, axis, [(i, (i + 2 * distance) % count) for i in range(count)])


def passed_on(x, axis):
    count = lax.axis_size(axis)
    return lax.ppermute(x, axis, [(i, i + 1) for i in range(count - 1)])


def local(density, active, neighbours, near_blocks, to_moments, from_moments, decay_rates, lengths):
    steps = density.shape[0]
    slabs, chips = lax.axis_size("tm"), lax.axis_size("space") // 2
    window, pair, other, far, decay, ends, live = prep(
        density,
        active.reshape(1, steps),
        to_moments,
        decay_rates.reshape(1, -1),
        lengths.reshape(1, steps),
        slabs,
    )
    ends = exchanged(ends, "tm")
    from_pair = swapped_from(pair, "space", 0)
    from_other = swapped_from(other, "space", 1)
    neighbours = neighbours.T
    inner = inner_near(neighbours, window, near_blocks)
    ends, inner = lax.optimization_barrier((ends, inner))
    mine = arrive(ends, far, decay)
    mine = pair_sum(mine, swapped_from(mine, "space", 0))
    parts = [mine] + [from_chip(mine, "space", d) for d in range(1, chips)]
    inner, mine = lax.optimization_barrier((inner, mine))
    near, carry, maps, _ = outer_near(
        neighbours, window, from_pair, from_other, near_blocks, inner, from_moments
    )
    carry = passed_on(carry, "tm")
    return final(near, carry, parts, maps, live)


def solution(mesh):
    placed = (
        P("tm", "space", None),
        P("tm"),
        P("space", None),
        P(None, "space", None, None, None),
        P(None, "space", None),
        P(None, "space", None),
        P(),
        P("tm"),
    )
    return jax.shard_map(
        local, mesh=mesh, in_specs=placed, out_specs=P("tm", "space", None), check_vma=False
    )
```

```python
import functools

import jax
import jax.numpy as jnp
from jax import lax
from jax.experimental import pallas as pl
from jax.experimental.pallas import tpu as pltpu
from jax.sharding import PartitionSpec as P

REACH = 8
F32 = jnp.float32
BF16 = jnp.bfloat16
HBM = pl.BlockSpec(memory_space=pltpu.HBM)
VMEM = pl.BlockSpec(memory_space=pltpu.VMEM)


def in_hbm(x):
    return pltpu.with_memory_space_constraint(x, pltpu.HBM)


def in_vmem(x):
    return pltpu.with_memory_space_constraint(x, pltpu.VMEM)


def column(row, lanes):
    return jnp.transpose(jnp.broadcast_to(row, (lanes, row.shape[1])))


def shifted_down(v, steps, fill):
    rows = v.shape[0]
    if steps < 8:
        moved = pltpu.roll(v, steps, 0)
        at = lax.broadcasted_iota(jnp.int32, v.shape, 0)
        return jnp.where(at < steps, jnp.full_like(v, fill), moved)
    return jnp.concatenate([jnp.full((steps, v.shape[1]), fill, v.dtype), v[: rows - steps]], 0)


def doubled(row):
    return jnp.concatenate([row, row], axis=1)


def is_even():
    return lax.rem(lax.axis_index("space"), 2) == 0


def prep_kernel(
    density,
    active,
    to_moments,
    rates,
    lengths,
    window,
    pair,
    other,
    far,
    decay,
    ends,
    live,
    dense,
    maps,
    active_row,
    rates_row,
    lengths_row,
    flat,
    lines,
    sems,
):
    steps, clusters, unknowns = density.shape
    terms = to_moments.shape[0]
    pieces = 4
    size = steps // pieces
    chunk = 32
    pitch = clusters + 1
    first = lax.axis_index("space") * clusters

    def copy(src, dst, k):
        return pltpu.make_async_copy(src, dst, sems.at[k])

    small = [
        copy(active, active_row, 0),
        copy(lengths, lengths_row, 1),
        copy(rates, rates_row, 2),
    ]
    parts = [
        copy(density.at[pl.ds(k * size, size)], dense.at[pl.ds(k * size, size)], 4 + k)
        for k in range(pieces)
    ]
    weights = copy(to_moments, maps, 3)
    for c in small + parts + [weights]:
        c.start()
    for c in small:
        c.wait()
    live[...] = column(active_row[...], unknowns)

    for k in range(pieces):
        parts[k].wait()

        def spread(i, _):
            start = pl.multiple_of(k * size + i * chunk, chunk)
            here = pl.ds(start, chunk)
            x = dense[here].astype(F32)
            for t in range(chunk):
                flat[pl.ds(t * pitch, clusters), :] = x[t]
            alive = live[here, :]
            for c in range(clusters):
                y = flat[pl.ds(c, chunk, stride=pitch), :]
                y = jnp.where(alive > first + c, y, 0.0)
                window[REACH + c, here, :] = y.astype(BF16)
            return 0

        lax.fori_loop(0, size // chunk, spread, 0)

    even = is_even()
    above = clusters
    sides = [
        copy(window.at[pl.ds(jnp.where(even, above, REACH), REACH)], pair, 8),
        copy(window.at[pl.ds(jnp.where(even, REACH, above), REACH)], other, 9),
    ]
    for c in sides:
        c.start()

    weights.wait()
    w = jnp.transpose(maps[...], (1, 0, 2))
    total = jnp.zeros((steps, 2 * terms), F32)
    for c in range(0, clusters, 2):
        x = jnp.concatenate([window[REACH + c], window[REACH + c + 1]], axis=1)
        y = jnp.concatenate([w[c], w[c + 1]], axis=1)
        y = jnp.concatenate([y, y], axis=0)
        total = total + lax.dot_general(
            x, y, (((1,), (1,)), ((), ())), preferred_element_type=F32
        )
    d = jnp.exp(-doubled(rates_row[...]) * column(lengths_row[...], 2 * terms))
    s = 1
    while s < steps:
        before = shifted_down(total, s, 0.0)
        factor = shifted_down(d, s, 1.0)
        total = total + d * before
        d = d * factor
        s *= 2
    lane = lax.broadcasted_iota(jnp.int32, (1, 2 * terms), 1)
    line = jnp.where(lane < terms, total[steps - 1 :], d[steps - 1 :])
    for k in range(ends.shape[0]):
        lines[k] = line
    sides.append(copy(lines, ends, 10))
    sides[-1].start()
    scale = jnp.sqrt(2.0 * doubled(rates_row[...]))
    far[...] = shifted_down(total, 1, 0.0) * scale
    decay[...] = shifted_down(d, 1, 1.0) * scale
    for c in sides:
        c.wait()


def prep(density, active, to_moments, rates, lengths, slabs):
    steps, clusters, unknowns = density.shape
    terms = to_moments.shape[0]
    lanes = 2 * terms
    side = pltpu.HBM((REACH, steps, unknowns), BF16)
    return pl.pallas_call(
        prep_kernel,
        in_specs=[HBM] * 5,
        out_specs=[VMEM, HBM, HBM, VMEM, VMEM, HBM, VMEM],
        out_shape=[
            jax.ShapeDtypeStruct((clusters + 2 * REACH, steps, unknowns), BF16),
            side,
            side,
            jax.ShapeDtypeStruct((steps, lanes), F32),
            jax.ShapeDtypeStruct((steps, lanes), F32),
            pltpu.HBM((slabs, 1, lanes), F32),
            jax.ShapeDtypeStruct((steps, unknowns), jnp.int32),
        ],
        scratch_shapes=[
            pltpu.VMEM(density.shape, BF16),
            pltpu.VMEM(to_moments.shape, BF16),
            pltpu.VMEM(active.shape, jnp.int32),
            pltpu.VMEM(rates.shape, F32),
            pltpu.VMEM(lengths.shape, F32),
            pltpu.VMEM((32 * (clusters + 1) + 7, unknowns), F32),
            pltpu.VMEM((slabs, 1, lanes), F32),
            pltpu.SemaphoreType.DMA((11,)),
        ],
        compiler_params=pltpu.CompilerParams(vmem_limit_bytes=10 << 20),
        name="prep",
    )(*map(in_hbm, (density, active, to_moments, rates, lengths)))


def arrive_kernel(ends, far, decay, out):
    me = lax.axis_index("tm")
    slabs = ends.shape[0]
    steps, lanes = far.shape
    half = lanes // 2
    lane = lax.broadcasted_iota(jnp.int32, (1, lanes), 1)
    state = jnp.zeros((1, lanes), F32)
    for k in range(slabs):
        v = ends[k]
        swapped = pltpu.roll(v, half, 1)
        end = jnp.where(lane < half, v, swapped)
        factor = jnp.where(lane < half, swapped, v)
        state = jnp.where(k < me, factor * state + end, state)
    x = far[...] + decay[...] * state
    wide = lax.broadcasted_iota(jnp.int32, (steps // 2, lanes), 1)
    out[...] = jnp.where(wide < half, x[: steps // 2], x[steps // 2 :])


def arrive(ends, far, decay):
    steps, lanes = far.shape
    return pl.pallas_call(
        arrive_kernel,
        in_specs=[VMEM] * 3,
        out_specs=VMEM,
        out_shape=jax.ShapeDtypeStruct((steps // 2, lanes), F32),
        compiler_params=pltpu.CompilerParams(vmem_limit_bytes=4 << 20),
        cost_estimate=pl.CostEstimate(
            flops=10_000_000_000, bytes_accessed=1 << 20, transcendentals=0
        ),
        name="arrive",
    )(ends, far, decay)


def pair_kernel(a, b, out):
    out[...] = (a[...] + b[...]).astype(BF16)


def pair_sum(a, b):
    return pl.pallas_call(
        pair_kernel,
        in_specs=[VMEM] * 2,
        out_specs=VMEM,
        out_shape=jax.ShapeDtypeStruct(a.shape, BF16),
        compiler_params=pltpu.CompilerParams(vmem_limit_bytes=4 << 20),
        name="pair_sum",
    )(a, b)


def gathered(neighbours, window, cluster, rows):
    base = lax.axis_index("space") * neighbours.shape[1] - REACH
    return jnp.concatenate(
        [window[neighbours[j, cluster] - base, rows, :] for j in range(neighbours.shape[0])], axis=1
    )


def stacked(block):
    nb, unknowns, width = block.shape
    return block[...].reshape(nb * unknowns, width)


def near_of(neighbours, window, blocks, cluster):
    steps = window.shape[1]
    x = gathered(neighbours, window, cluster, pl.ds(0, steps))
    w = jnp.concatenate([stacked(block) for block in blocks], axis=1)
    both = jnp.dot(x, w, preferred_element_type=F32)
    now, later = jnp.split(both, 2, axis=1)
    return now + shifted_down(later, 1, 0.0), later[steps - 1 :]


def inner_kernel(
    full,
    ends_only,
    table,
    window,
    blocks,
    near,
    carry,
    neighbours,
    held,
    held_later,
    found,
    lines,
    sems,
    later_sems,
    out_sems,
):
    count = len(full)
    steps = window.shape[1]
    lags = blocks.shape[0]
    fetches = [
        [
            pltpu.make_async_copy(blocks.at[lag, c], held.at[lag, i], sems.at[lag, i])
            for lag in range(lags)
        ]
        for i, c in enumerate(full)
    ]
    later_fetches = [
        pltpu.make_async_copy(blocks.at[lags - 1, c], held_later.at[i], later_sems.at[i])
        for i, c in enumerate(ends_only)
    ]
    listed = pltpu.make_async_copy(table, neighbours, out_sems.at[count + 1])
    listed.start()
    for some in fetches:
        for fetch in some:
            fetch.start()
    for fetch in later_fetches:
        fetch.start()
    listed.wait()
    stores = []
    for i, cluster in enumerate(full):
        for fetch in fetches[i]:
            fetch.wait()
        blocks_here = [held.at[lag, i] for lag in range(lags)]
        x, last = near_of(neighbours, window, blocks_here, cluster)
        found[i] = x
        lines[cluster - REACH] = last
        stores.append(pltpu.make_async_copy(found.at[i], near.at[i], out_sems.at[i]))
        stores[-1].start()
    for i, cluster in enumerate(ends_only):
        later_fetches[i].wait()
        x = gathered(neighbours, window, cluster, pl.ds(steps - 16, 16))
        y = jnp.dot(x, stacked(held_later.at[i]), preferred_element_type=F32)
        lines[cluster - REACH] = y[15:]
    stores.append(pltpu.make_async_copy(lines, carry, out_sems.at[count]))
    stores[-1].start()
    for store in stores:
        store.wait()


def inner_near(neighbours, window, blocks, full, ends_only):
    steps, unknowns = window.shape[1:]
    lags, clusters, nb = blocks.shape[:3]
    count, more = len(full), len(ends_only)
    block = (nb, unknowns, unknowns)
    return pl.pallas_call(
        functools.partial(inner_kernel, full, ends_only),
        in_specs=[HBM, VMEM, HBM],
        out_specs=[HBM] * 2,
        out_shape=[
            pltpu.HBM((count, steps, unknowns), F32),
            pltpu.HBM((count + more, 1, unknowns), F32),
        ],
        scratch_shapes=[
            pltpu.SMEM(neighbours.shape, jnp.int32),
            pltpu.VMEM((lags, count, *block), BF16),
            pltpu.VMEM((more, *block), BF16),
            pltpu.VMEM((count, steps, unknowns), F32),
            pltpu.VMEM((count + more, 1, unknowns), F32),
            pltpu.SemaphoreType.DMA((lags, count)),
            pltpu.SemaphoreType.DMA((more,)),
            pltpu.SemaphoreType.DMA((count + 2,)),
        ],
        compiler_params=pltpu.CompilerParams(vmem_limit_bytes=16 << 20),
        name="inner",
    )(in_hbm(neighbours), window, in_hbm(blocks))


def edge_kernel(
    order,
    table,
    window_in,
    from_pair,
    from_other,
    blocks,
    inner_carry,
    near,
    carry,
    window,
    neighbours,
    sems,
):
    del window_in
    even = is_even()
    above = window.shape[0] - REACH

    def copy(src, dst, k):
        return pltpu.make_async_copy(src, dst, sems.at[k])

    sides = [
        copy(from_pair, window.at[pl.ds(jnp.where(even, above, 0), REACH)], 0),
        copy(from_other, window.at[pl.ds(jnp.where(even, 0, above), REACH)], 1),
        copy(inner_carry, carry.at[pl.ds(REACH, inner_carry.shape[0])], 2),
        copy(table, neighbours, 3),
    ]
    for c in sides:
        c.start()
    for c in sides:
        c.wait()
    for i, cluster in enumerate(order):
        blocks_here = [blocks.at[lag, cluster] for lag in range(blocks.shape[0])]
        near[i], carry[cluster] = near_of(neighbours, window, blocks_here, cluster)


def edge_near(neighbours, window, from_pair, from_other, blocks, inner_carry, order):
    steps, unknowns = window.shape[1:]
    clusters = blocks.shape[1]
    return pl.pallas_call(
        functools.partial(edge_kernel, order),
        in_specs=[HBM, VMEM, HBM, HBM, VMEM, HBM],
        out_specs=[VMEM] * 3,
        out_shape=[
            jax.ShapeDtypeStruct((len(order), steps, unknowns), F32),
            jax.ShapeDtypeStruct((clusters, 1, unknowns), F32),
            jax.ShapeDtypeStruct(window.shape, BF16),
        ],
        scratch_shapes=[
            pltpu.SMEM(neighbours.shape, jnp.int32),
            pltpu.SemaphoreType.DMA((4,)),
        ],
        input_output_aliases={1: 2},
        compiler_params=pltpu.CompilerParams(vmem_limit_bytes=8 << 20),
        name="edge",
    )(
        in_hbm(neighbours),
        window,
        in_hbm(from_pair),
        in_hbm(from_other),
        in_vmem(blocks),
        in_hbm(inner_carry),
    )


def rest_kernel(
    order, table, window, blocks, inner, from_moments, near, maps, neighbours, rows, sems
):
    listed = pltpu.make_async_copy(table, neighbours, sems.at[2])
    listed.start()
    fetches = [
        pltpu.make_async_copy(from_moments, rows, sems.at[0]),
        pltpu.make_async_copy(inner, near.at[pl.ds(len(order), inner.shape[0])], sems.at[1]),
    ]
    for fetch in fetches:
        fetch.start()
    listed.wait()
    for i, cluster in enumerate(order):
        blocks_here = [blocks.at[lag, cluster] for lag in range(blocks.shape[0])]
        near[i], _ = near_of(neighbours, window, blocks_here, cluster)
    fetches[0].wait()
    w = jnp.transpose(rows[...], (1, 0, 2))
    for p in range(maps.shape[0]):
        x = jnp.concatenate([w[2 * p], w[2 * p + 1]], axis=1)
        maps[p] = jnp.concatenate([x, x], axis=0)
    fetches[1].wait()


def rest_near(neighbours, window, blocks, inner, from_moments, order):
    steps, unknowns = window.shape[1:]
    clusters = blocks.shape[1]
    terms = from_moments.shape[0]
    return pl.pallas_call(
        functools.partial(rest_kernel, order),
        in_specs=[HBM, VMEM, VMEM, HBM, HBM],
        out_specs=[VMEM] * 2,
        out_shape=[
            jax.ShapeDtypeStruct((len(order) + inner.shape[0], steps, unknowns), F32),
            jax.ShapeDtypeStruct((clusters // 2, 2 * terms, 2 * unknowns), BF16),
        ],
        scratch_shapes=[
            pltpu.SMEM(neighbours.shape, jnp.int32),
            pltpu.VMEM(from_moments.shape, BF16),
            pltpu.SemaphoreType.DMA((3,)),
        ],
        compiler_params=pltpu.CompilerParams(vmem_limit_bytes=8 << 20),
        name="rest",
    )(in_hbm(neighbours), window, in_vmem(blocks), in_hbm(inner), in_hbm(from_moments))


def final_kernel(places, edge, rest, carry, *refs):
    parts = refs[:4]
    maps, live, out, major, done, sems = refs[4:]
    steps, clusters, unknowns = out.shape
    terms = maps.shape[1] // 2
    first = lax.axis_index("space") * clusters
    total = parts[0][...].astype(F32)
    for part in parts[1:]:
        total = total + part[...].astype(F32)
    lane = lax.broadcasted_iota(jnp.int32, total.shape, 1)
    size = steps // 2
    chunk = 32
    row = lax.broadcasted_iota(jnp.int32, (8, unknowns), 0)
    copies = []
    for half in range(2):
        mine = jnp.where(lane // terms == half, total, 0.0).astype(BF16)
        here = pl.ds(half * size, size)
        alive = live[here, :]
        for p in range(clusters // 2):
            both = jnp.dot(mine, maps[p], preferred_element_type=F32)
            for q in range(2):
                c = 2 * p + q
                which, at = places[c]
                near = (edge, rest)[which]
                x = both[:, q * unknowns : (q + 1) * unknowns] + near[at, here, :]
                if half == 0:
                    head = jnp.where(row == 0, jnp.broadcast_to(carry[c], row.shape), 0.0)
                    x = jnp.concatenate([x[:8] + head, x[8:]], axis=0)
                major[c] = jnp.where(alive > first + c, x, 0.0).astype(BF16)
        for i in range(size // chunk):
            start = half * size + i * chunk
            rows = pl.ds(start, chunk)
            done[rows] = jnp.transpose(major[:, pl.ds(i * chunk, chunk), :], (1, 0, 2))
            copies.append(
                pltpu.make_async_copy(done.at[rows], out.at[rows], sems.at[start // chunk])
            )
            copies[-1].start()
    for copy in copies:
        copy.wait()


def final(edge, rest, carry, parts, maps, live, orders):
    steps, unknowns = live.shape
    clusters = carry.shape[0]
    places = {c: (k, i) for k, order in enumerate(orders) for i, c in enumerate(order)}
    return pl.pallas_call(
        functools.partial(final_kernel, places),
        in_specs=[VMEM] * (5 + len(parts)),
        out_specs=HBM,
        out_shape=jax.ShapeDtypeStruct((steps, clusters, unknowns), BF16),
        scratch_shapes=[
            pltpu.VMEM((clusters, steps // 2, unknowns), BF16),
            pltpu.VMEM((steps, clusters, unknowns), BF16),
            pltpu.SemaphoreType.DMA((steps // 32,)),
        ],
        compiler_params=pltpu.CompilerParams(vmem_limit_bytes=10 << 20),
        name="final",
    )(edge, rest, carry, *parts, maps, live)


def exchanged(x, axis):
    return lax.all_to_all(x, axis, split_axis=0, concat_axis=0, tiled=True)


def swapped_from(x, axis, start):
    count = lax.axis_size(axis)
    route = []
    for i in range(start, count - 1, 2):
        route += [(i, i + 1), (i + 1, i)]
    return lax.ppermute(x, axis, route)


def from_chip(x, axis, distance):
    count = lax.axis_size(axis)
    return lax.ppermute(x, axis, [(i, (i + 2 * distance) % count) for i in range(count)])


def passed_on(x, axis):
    count = lax.axis_size(axis)
    return lax.ppermute(x, axis, [(i, i + 1) for i in range(count - 1)])


def local(density, active, neighbours, near_blocks, to_moments, from_moments, decay_rates, lengths):
    steps = density.shape[0]
    slabs, chips = lax.axis_size("tm"), lax.axis_size("space") // 2
    window, pair, other, far, decay, ends, live = prep(
        density,
        active.reshape(1, steps),
        to_moments,
        decay_rates.reshape(1, -1),
        lengths.reshape(1, steps),
        slabs,
    )
    ends = exchanged(ends, "tm")
    from_pair = swapped_from(pair, "space", 0)
    from_other = swapped_from(other, "space", 1)
    neighbours = neighbours.T
    clusters = density.shape[1]
    middle = clusters // 2
    full = tuple(range(middle - REACH // 2, middle + REACH // 2))
    sides = tuple(range(REACH)) + tuple(range(clusters - REACH, clusters))
    others = tuple(c for c in range(clusters) if c not in full + sides)
    inner, inner_carry = inner_near(neighbours, window, near_blocks, full, others)
    ends, inner, inner_carry = lax.optimization_barrier((ends, inner, inner_carry))
    mine = arrive(ends, far, decay)
    mine = pair_sum(mine, swapped_from(mine, "space", 0))
    parts = [mine] + [from_chip(mine, "space", d) for d in range(1, chips)]
    inner_carry, mine = lax.optimization_barrier((inner_carry, mine))
    edge, carry, window = edge_near(
        neighbours, window, from_pair, from_other, near_blocks, inner_carry, sides
    )
    carry = passed_on(carry, "tm")
    rest, maps = rest_near(neighbours, window, near_blocks, inner, from_moments, others)
    return final(edge, rest, carry, parts, maps, live, (sides, others + full))


def solution(mesh):
    placed = (
        P("tm", "space", None),
        P("tm"),
        P("space", None),
        P(None, "space", None, None, None),
        P(None, "space", None),
        P(None, "space", None),
        P(),
        P("tm"),
    )
    return jax.shard_map(
        local, mesh=mesh, in_specs=placed, out_specs=P("tm", "space", None), check_vma=False
    )
```

```python
import functools

import jax
import jax.numpy as jnp
from jax import lax
from jax.experimental import pallas as pl
from jax.experimental.pallas import tpu as pltpu
from jax.sharding import PartitionSpec as P

REACH = 8
F32 = jnp.float32
BF16 = jnp.bfloat16
HBM = pl.BlockSpec(memory_space=pltpu.HBM)
VMEM = pl.BlockSpec(memory_space=pltpu.VMEM)
SMEM = pl.BlockSpec(memory_space=pltpu.SMEM)


def in_hbm(x):
    return pltpu.with_memory_space_constraint(x, pltpu.HBM)


def in_vmem(x):
    return pltpu.with_memory_space_constraint(x, pltpu.VMEM)


def column(row, lanes):
    return jnp.transpose(jnp.broadcast_to(row, (lanes, row.shape[1])))


def shifted_down(v, steps, fill):
    rows = v.shape[0]
    if steps < 8:
        moved = pltpu.roll(v, steps, 0)
        at = lax.broadcasted_iota(jnp.int32, v.shape, 0)
        return jnp.where(at < steps, jnp.full_like(v, fill), moved)
    return jnp.concatenate([jnp.full((steps, v.shape[1]), fill, v.dtype), v[: rows - steps]], 0)


def doubled(row):
    return jnp.concatenate([row, row], axis=1)


def is_even():
    return lax.rem(lax.axis_index("space"), 2) == 0


def prep_kernel(
    density,
    active,
    to_moments,
    rates,
    lengths,
    neighbours,
    window,
    far,
    decay,
    ends,
    live,
    table,
    dense,
    maps,
    active_row,
    rates_row,
    lengths_row,
    flat,
    sems,
):
    steps, clusters, unknowns = density.shape
    terms = to_moments.shape[0]
    pieces = 4
    size = steps // pieces
    chunk = 32
    pitch = clusters + 1
    first = lax.axis_index("space") * clusters

    def copy(src, dst, k):
        return pltpu.make_async_copy(src, dst, sems.at[k])

    small = [
        copy(active, active_row, 0),
        copy(lengths, lengths_row, 1),
        copy(rates, rates_row, 2),
    ]
    parts = [
        copy(density.at[pl.ds(k * size, size)], dense.at[pl.ds(k * size, size)], 4 + k)
        for k in range(pieces)
    ]
    weights = copy(to_moments, maps, 3)
    listed = copy(neighbours, table, 8)
    for c in small + parts + [weights, listed]:
        c.start()
    for c in small:
        c.wait()
    live[...] = column(active_row[...], unknowns)

    for k in range(pieces):
        parts[k].wait()

        def spread(i, _):
            start = pl.multiple_of(k * size + i * chunk, chunk)
            here = pl.ds(start, chunk)
            x = dense[here].astype(F32)
            for t in range(chunk):
                flat[pl.ds(t * pitch, clusters), :] = x[t]
            alive = live[here, :]
            for c in range(clusters):
                y = flat[pl.ds(c, chunk, stride=pitch), :]
                y = jnp.where(alive > first + c, y, 0.0)
                window[REACH + c, here, :] = y.astype(BF16)
            return 0

        lax.fori_loop(0, size // chunk, spread, 0)

    weights.wait()
    w = jnp.transpose(maps[...], (1, 0, 2))
    total = jnp.zeros((steps, 2 * terms), F32)
    for c in range(0, clusters, 2):
        x = jnp.concatenate([window[REACH + c], window[REACH + c + 1]], axis=1)
        y = jnp.concatenate([w[c], w[c + 1]], axis=1)
        y = jnp.concatenate([y, y], axis=0)
        total = total + lax.dot_general(
            x, y, (((1,), (1,)), ((), ())), preferred_element_type=F32
        )
    d = jnp.exp(-doubled(rates_row[...]) * column(lengths_row[...], 2 * terms))
    s = 1
    while s < steps:
        before = shifted_down(total, s, 0.0)
        factor = shifted_down(d, s, 1.0)
        total = total + d * before
        d = d * factor
        s *= 2
    lane = lax.broadcasted_iota(jnp.int32, (1, 2 * terms), 1)
    line = jnp.where(lane < terms, total[steps - 1 :], d[steps - 1 :])
    ends[...] = line
    scale = jnp.sqrt(2.0 * doubled(rates_row[...]))
    far[...] = shifted_down(total, 1, 0.0) * scale
    decay[...] = shifted_down(d, 1, 1.0) * scale
    listed.wait()


def prep(density, active, to_moments, rates, lengths, neighbours):
    steps, clusters, unknowns = density.shape
    terms = to_moments.shape[0]
    lanes = 2 * terms
    return pl.pallas_call(
        prep_kernel,
        in_specs=[HBM] * 6,
        out_specs=[VMEM] * 6,
        out_shape=[
            jax.ShapeDtypeStruct((clusters + 2 * REACH, steps, unknowns), BF16),
            jax.ShapeDtypeStruct((steps, lanes), F32),
            jax.ShapeDtypeStruct((steps, lanes), F32),
            jax.ShapeDtypeStruct((1, lanes), F32),
            jax.ShapeDtypeStruct((steps, unknowns), jnp.int32),
            jax.ShapeDtypeStruct(neighbours.shape, jnp.int32),
        ],
        scratch_shapes=[
            pltpu.VMEM(density.shape, BF16),
            pltpu.VMEM(to_moments.shape, BF16),
            pltpu.VMEM(active.shape, jnp.int32),
            pltpu.VMEM(rates.shape, F32),
            pltpu.VMEM(lengths.shape, F32),
            pltpu.VMEM((32 * (clusters + 1) + 7, unknowns), F32),
            pltpu.SemaphoreType.DMA((9,)),
        ],
        compiler_params=pltpu.CompilerParams(vmem_limit_bytes=8 << 20),
        cost_estimate=pl.CostEstimate(
            flops=12_000_000_000, bytes_accessed=1 << 20, transcendentals=0
        ),
        name="prep",
    )(*map(in_hbm, (density, active, to_moments, rates, lengths, neighbours)))


def sides_kernel(window, pair, other):
    even = is_even()
    above = window.shape[0] - 2 * REACH
    pair[...] = window[pl.ds(jnp.where(even, above, REACH), REACH)]
    other[...] = window[pl.ds(jnp.where(even, REACH, above), REACH)]


def sides_of(window):
    side = jax.ShapeDtypeStruct((REACH, *window.shape[1:]), BF16)
    return pl.pallas_call(
        sides_kernel,
        in_specs=[VMEM],
        out_specs=[VMEM] * 2,
        out_shape=[side, side],
        compiler_params=pltpu.CompilerParams(vmem_limit_bytes=1 << 20),
        name="sides",
    )(window)


def after(first, second):
    lanes = first.shape[1]
    half = lanes // 2
    lane = lax.broadcasted_iota(jnp.int32, first.shape, 1)
    factor = jnp.where(lane < half, pltpu.roll(second, half, 1), second)
    return factor * first + jnp.where(lane < half, second, 0.0)


def fold_kernel(bit, own, arriving, seen, whole, before):
    upper = lax.rem(lax.axis_index("tm") // bit, 2) == 1
    mine, theirs, past = own[...], seen[...], arriving[...]
    first = jnp.where(upper, theirs, mine)
    second = jnp.where(upper, mine, theirs)
    whole[...] = after(first, second)
    before[...] = jnp.where(upper, after(theirs, past), past)


def fold(bit, own, arriving, seen):
    line = jax.ShapeDtypeStruct(own.shape, F32)
    return pl.pallas_call(
        functools.partial(fold_kernel, bit),
        in_specs=[VMEM] * 3,
        out_specs=[VMEM] * 2,
        out_shape=[line, line],
        compiler_params=pltpu.CompilerParams(vmem_limit_bytes=1 << 20),
        name="fold",
    )(own, arriving, seen)


def arrive_kernel(before, far, decay, out):
    steps, lanes = far.shape
    half = lanes // 2
    line = before[...]
    lane = lax.broadcasted_iota(jnp.int32, line.shape, 1)
    state = jnp.where(lane < half, line, pltpu.roll(line, half, 1))
    x = far[...] + decay[...] * state
    wide = lax.broadcasted_iota(jnp.int32, (steps // 2, lanes), 1)
    out[...] = jnp.where(wide < half, x[: steps // 2], x[steps // 2 :])


def arrive(before, far, decay):
    steps, lanes = far.shape
    return pl.pallas_call(
        arrive_kernel,
        in_specs=[VMEM] * 3,
        out_specs=VMEM,
        out_shape=jax.ShapeDtypeStruct((steps // 2, lanes), F32),
        compiler_params=pltpu.CompilerParams(vmem_limit_bytes=4 << 20),
        name="arrive",
    )(before, far, decay)


def pair_kernel(a, b, out):
    out[...] = (a[...] + b[...]).astype(BF16)


def pair_sum(a, b):
    return pl.pallas_call(
        pair_kernel,
        in_specs=[VMEM] * 2,
        out_specs=VMEM,
        out_shape=jax.ShapeDtypeStruct(a.shape, BF16),
        compiler_params=pltpu.CompilerParams(vmem_limit_bytes=4 << 20),
        name="pair_sum",
    )(a, b)


def gathered(neighbours, window, cluster, rows):
    base = lax.axis_index("space") * neighbours.shape[1] - REACH
    return jnp.concatenate(
        [window[neighbours[j, cluster] - base, rows, :] for j in range(neighbours.shape[0])], axis=1
    )


def stacked(block):
    nb, unknowns, width = block.shape
    return block[...].reshape(nb * unknowns, width)


def near_of(neighbours, window, blocks, cluster):
    steps = window.shape[1]
    x = gathered(neighbours, window, cluster, pl.ds(0, steps))
    w = jnp.concatenate([stacked(block) for block in blocks], axis=1)
    both = jnp.dot(x, w, preferred_element_type=F32)
    now, later = jnp.split(both, 2, axis=1)
    return now + shifted_down(later, 1, 0.0), later[steps - 1 :]


def inner_kernel(order, neighbours, window, blocks, near, carry):
    for i, cluster in enumerate(order):
        blocks_here = [blocks.at[lag, cluster] for lag in range(blocks.shape[0])]
        near[i], carry[i] = near_of(neighbours, window, blocks_here, cluster)


def mapped_kernel(order, neighbours, window, blocks, from_moments, near, carry, maps, rows, sems):
    fetch = pltpu.make_async_copy(from_moments, rows, sems.at[0])
    fetch.start()
    inner_kernel(order, neighbours, window, blocks, near, carry)
    fetch.wait()
    w = jnp.transpose(rows[...], (1, 0, 2))
    for p in range(maps.shape[0]):
        x = jnp.concatenate([w[2 * p], w[2 * p + 1]], axis=1)
        maps[p] = jnp.concatenate([x, x], axis=0)


def joined_kernel(
    order, neighbours, window_in, from_pair, from_other, blocks, near, carry, window
):
    del window_in
    even = is_even()
    above = window.shape[0] - REACH
    window[pl.ds(jnp.where(even, above, 0), REACH)] = from_pair[...]
    window[pl.ds(jnp.where(even, 0, above), REACH)] = from_other[...]
    inner_kernel(order, neighbours, window, blocks, near, carry)


def last_kernel(order, neighbours, window, blocks, *refs):
    earlier = refs[:-3]
    near, carry, lines = refs[-3:]
    inner_kernel(order, neighbours, window, blocks, near, carry)
    for k, ref in enumerate(earlier + (carry,)):
        for i in range(len(order)):
            lines[k * len(order) + i] = ref[i]


def near_call(body, order, operands, specs, window, blocks, more=(), scratch=(), aliases={}):
    steps, unknowns = window.shape[1:]
    shapes = [
        jax.ShapeDtypeStruct((len(order), steps, unknowns), F32),
        jax.ShapeDtypeStruct((len(order), 1, unknowns), F32),
        *more,
    ]
    return pl.pallas_call(
        functools.partial(body, order),
        in_specs=[SMEM] + specs,
        out_specs=[VMEM] * len(shapes),
        out_shape=shapes,
        scratch_shapes=list(scratch),
        input_output_aliases=aliases,
        compiler_params=pltpu.CompilerParams(vmem_limit_bytes=4 << 20),
        name="near",
    )(*operands)


def final_kernel(orders, *refs):
    groups = len(orders)
    nears, carry, parts = refs[:groups], refs[groups], refs[groups + 1 : -6]
    maps, live, out, major, done, sems = refs[-6:]
    places = {c: (k, i) for k, order in enumerate(orders) for i, c in enumerate(order)}
    steps, clusters, unknowns = out.shape
    terms = maps.shape[1] // 2
    first = lax.axis_index("space") * clusters
    total = parts[0][...].astype(F32)
    for part in parts[1:]:
        total = total + part[...].astype(F32)
    lane = lax.broadcasted_iota(jnp.int32, total.shape, 1)
    size = steps // 2
    chunk = 32
    row = lax.broadcasted_iota(jnp.int32, (8, unknowns), 0)
    copies = []
    for half in range(2):
        mine = jnp.where(lane // terms == half, total, 0.0).astype(BF16)
        here = pl.ds(half * size, size)
        alive = live[here, :]
        for p in range(clusters // 2):
            both = jnp.dot(mine, maps[p], preferred_element_type=F32)
            for q in range(2):
                c = 2 * p + q
                k, i = places[c]
                x = both[:, q * unknowns : (q + 1) * unknowns] + nears[k][i, here, :]
                if half == 0:
                    head = jnp.where(row == 0, jnp.broadcast_to(carry[k * REACH + i], row.shape), 0.0)
                    x = jnp.concatenate([x[:8] + head, x[8:]], axis=0)
                major[c] = jnp.where(alive > first + c, x, 0.0).astype(BF16)
        for i in range(size // chunk):
            start = half * size + i * chunk
            rows = pl.ds(start, chunk)
            done[rows] = jnp.transpose(major[:, pl.ds(i * chunk, chunk), :], (1, 0, 2))
            copies.append(
                pltpu.make_async_copy(done.at[rows], out.at[rows], sems.at[start // chunk])
            )
            copies[-1].start()
    for copy in copies:
        copy.wait()


def final(orders, nears, carry, parts, maps, live):
    steps, unknowns = live.shape
    clusters = carry.shape[0]
    return pl.pallas_call(
        functools.partial(final_kernel, orders),
        in_specs=[VMEM] * (len(nears) + len(parts) + 3),
        out_specs=HBM,
        out_shape=jax.ShapeDtypeStruct((steps, clusters, unknowns), BF16),
        scratch_shapes=[
            pltpu.VMEM((clusters, steps // 2, unknowns), BF16),
            pltpu.VMEM((steps, clusters, unknowns), BF16),
            pltpu.SemaphoreType.DMA((steps // 32,)),
        ],
        compiler_params=pltpu.CompilerParams(vmem_limit_bytes=10 << 20),
        name="final",
    )(*nears, carry, *parts, maps, live)


def across(x, axis, bit):
    count = lax.axis_size(axis)
    return lax.ppermute(x, axis, [(i, i ^ bit) for i in range(count)])


def swapped_from(x, axis, start):
    count = lax.axis_size(axis)
    route = []
    for i in range(start, count - 1, 2):
        route += [(i, i + 1), (i + 1, i)]
    return lax.ppermute(x, axis, route)


def from_chip(x, axis, distance):
    count = lax.axis_size(axis)
    return lax.ppermute(x, axis, [(i, (i + 2 * distance) % count) for i in range(count)])


def passed_on(x, axis):
    count = lax.axis_size(axis)
    return lax.ppermute(x, axis, [(i, i + 1) for i in range(count - 1)])


def local(density, active, neighbours, near_blocks, to_moments, from_moments, decay_rates, lengths):
    steps, clusters, unknowns = density.shape
    terms = decay_rates.shape[0]
    chips = lax.axis_size("space") // 2
    window, far, decay, own, live, table = prep(
        density,
        active.reshape(1, steps),
        to_moments,
        decay_rates.reshape(1, -1),
        lengths.reshape(1, steps),
        neighbours.T,
    )
    half = clusters // 2
    orders = (
        tuple(range(REACH, half)),
        tuple(range(half, clusters - REACH)),
        tuple(range(REACH)),
        tuple(range(clusters - REACH, clusters)),
    )
    blocks = in_vmem(near_blocks)
    maps_shape = jax.ShapeDtypeStruct((clusters // 2, 2 * terms, 2 * unknowns), BF16)
    bits = [1 << k for k in range((lax.axis_size("tm") - 1).bit_length())]
    nears, carries = [], []
    lane = lax.broadcasted_iota(jnp.int32, own.shape, 1)
    arriving = jnp.where(lane < terms, 0.0, 1.0)
    pair, other = sides_of(window)
    from_pair = swapped_from(pair, "space", 0)
    from_other = swapped_from(other, "space", 1)
    for turn, bit in enumerate(bits):
        seen = across(own, "tm", bit)
        if turn < len(orders):
            order = orders[turn]
            table, own = lax.optimization_barrier((table, own))
            if turn == 0:
                near, carry, maps = near_call(
                    mapped_kernel,
                    order,
                    (table, window, blocks, in_hbm(from_moments)),
                    [VMEM, VMEM, HBM],
                    window,
                    blocks,
                    (maps_shape,),
                    (
                        pltpu.VMEM(from_moments.shape, BF16),
                        pltpu.SemaphoreType.DMA((1,)),
                    ),
                )
            elif turn == 1:
                near, carry = near_call(
                    inner_kernel, order, (table, window, blocks), [VMEM] * 2, window, blocks
                )
            elif turn == 2:
                near, carry, window = near_call(
                    joined_kernel,
                    order,
                    (table, window, from_pair, from_other, blocks),
                    [VMEM] * 4,
                    window,
                    blocks,
                    (jax.ShapeDtypeStruct(window.shape, BF16),),
                    aliases={1: 2},
                )
            else:
                near, carry, lines = near_call(
                    last_kernel,
                    order,
                    (table, window, blocks, *carries),
                    [VMEM] * (2 + len(carries)),
                    window,
                    blocks,
                    (jax.ShapeDtypeStruct((clusters, 1, unknowns), F32),),
                )
            nears.append(near)
            carries.append(carry)
            if turn < len(orders) - 1:
                seen, carry = lax.optimization_barrier((seen, carry))
            else:
                seen, lines = lax.optimization_barrier((seen, lines))
        own, arriving = fold(bit, own, arriving, seen)
    lines = passed_on(lines, "tm")
    mine = arrive(arriving, far, decay)
    mine = pair_sum(mine, swapped_from(mine, "space", 0))
    parts = [mine] + [from_chip(mine, "space", d) for d in range(1, chips)]
    return final(orders, nears, lines, parts, maps, live)


def solution(mesh):
    placed = (
        P("tm", "space", None),
        P("tm"),
        P("space", None),
        P(None, "space", None, None, None),
        P(None, "space", None),
        P(None, "space", None),
        P(),
        P("tm"),
    )
    return jax.shard_map(
        local, mesh=mesh, in_specs=placed, out_specs=P("tm", "space", None), check_vma=False
    )
```

```python
import functools

import jax
import jax.numpy as jnp
from jax import lax
from jax.experimental import pallas as pl
from jax.experimental.pallas import tpu as pltpu
from jax.sharding import PartitionSpec as P

REACH = 8
F32 = jnp.float32
BF16 = jnp.bfloat16
HBM = pl.BlockSpec(memory_space=pltpu.HBM)
VMEM = pl.BlockSpec(memory_space=pltpu.VMEM)


def in_hbm(x):
    return pltpu.with_memory_space_constraint(x, pltpu.HBM)


def in_vmem(x):
    return pltpu.with_memory_space_constraint(x, pltpu.VMEM)


def column(row, lanes):
    return jnp.transpose(jnp.broadcast_to(row, (lanes, row.shape[1])))


def shifted_down(v, steps, fill):
    rows = v.shape[0]
    if steps < 8:
        moved = pltpu.roll(v, steps, 0)
        at = lax.broadcasted_iota(jnp.int32, v.shape, 0)
        return jnp.where(at < steps, jnp.full_like(v, fill), moved)
    return jnp.concatenate([jnp.full((steps, v.shape[1]), fill, v.dtype), v[: rows - steps]], 0)


def doubled(row):
    return jnp.concatenate([row, row], axis=1)


def is_even():
    return lax.rem(lax.axis_index("space"), 2) == 0


def prep_kernel(
    density,
    active,
    to_moments,
    rates,
    lengths,
    window,
    pair,
    other,
    far,
    decay,
    ends,
    live,
    dense,
    maps,
    active_row,
    rates_row,
    lengths_row,
    flat,
    lines,
    sems,
):
    steps, clusters, unknowns = density.shape
    terms = to_moments.shape[0]
    pieces = 4
    size = steps // pieces
    chunk = 32
    pitch = clusters + 1
    first = lax.axis_index("space") * clusters

    def copy(src, dst, k):
        return pltpu.make_async_copy(src, dst, sems.at[k])

    small = [
        copy(active, active_row, 0),
        copy(lengths, lengths_row, 1),
        copy(rates, rates_row, 2),
    ]
    parts = [
        copy(density.at[pl.ds(k * size, size)], dense.at[pl.ds(k * size, size)], 4 + k)
        for k in range(pieces)
    ]
    weights = copy(to_moments, maps, 3)
    for c in small + parts + [weights]:
        c.start()
    for c in small:
        c.wait()
    live[...] = column(active_row[...], unknowns)

    for k in range(pieces):
        parts[k].wait()

        def spread(i, _):
            start = pl.multiple_of(k * size + i * chunk, chunk)
            here = pl.ds(start, chunk)
            x = dense[here].astype(F32)
            for t in range(chunk):
                flat[pl.ds(t * pitch, clusters), :] = x[t]
            alive = live[here, :]
            for c in range(clusters):
                y = flat[pl.ds(c, chunk, stride=pitch), :]
                y = jnp.where(alive > first + c, y, 0.0)
                window[REACH + c, here, :] = y.astype(BF16)
            return 0

        lax.fori_loop(0, size // chunk, spread, 0)

    even = is_even()
    above = clusters
    sides = [
        copy(window.at[pl.ds(jnp.where(even, above, REACH), REACH)], pair, 8),
        copy(window.at[pl.ds(jnp.where(even, REACH, above), REACH)], other, 9),
    ]
    for c in sides:
        c.start()

    weights.wait()
    w = jnp.transpose(maps[...], (1, 0, 2))
    total = jnp.zeros((steps, 2 * terms), F32)
    for c in range(0, clusters, 2):
        x = jnp.concatenate([window[REACH + c], window[REACH + c + 1]], axis=1)
        y = jnp.concatenate([w[c], w[c + 1]], axis=1)
        y = jnp.concatenate([y, y], axis=0)
        total = total + lax.dot_general(
            x, y, (((1,), (1,)), ((), ())), preferred_element_type=F32
        )
    d = jnp.exp(-doubled(rates_row[...]) * column(lengths_row[...], 2 * terms))
    s = 1
    while s < steps:
        before = shifted_down(total, s, 0.0)
        factor = shifted_down(d, s, 1.0)
        total = total + d * before
        d = d * factor
        s *= 2
    lane = lax.broadcasted_iota(jnp.int32, (1, 2 * terms), 1)
    line = jnp.where(lane < terms, total[steps - 1 :], d[steps - 1 :])
    for k in range(ends.shape[0]):
        lines[k] = line
    sides.append(copy(lines, ends, 10))
    sides[-1].start()
    scale = jnp.sqrt(2.0 * doubled(rates_row[...]))
    far[...] = shifted_down(total, 1, 0.0) * scale
    decay[...] = shifted_down(d, 1, 1.0) * scale
    for c in sides:
        c.wait()


def prep(density, active, to_moments, rates, lengths, slabs):
    steps, clusters, unknowns = density.shape
    terms = to_moments.shape[0]
    lanes = 2 * terms
    side = pltpu.HBM((REACH, steps, unknowns), BF16)
    return pl.pallas_call(
        prep_kernel,
        in_specs=[HBM] * 5,
        out_specs=[VMEM, HBM, HBM, VMEM, VMEM, HBM, VMEM],
        out_shape=[
            jax.ShapeDtypeStruct((clusters + 2 * REACH, steps, unknowns), BF16),
            side,
            side,
            jax.ShapeDtypeStruct((steps, lanes), F32),
            jax.ShapeDtypeStruct((steps, lanes), F32),
            pltpu.HBM((slabs, 1, lanes), F32),
            jax.ShapeDtypeStruct((steps, unknowns), jnp.int32),
        ],
        scratch_shapes=[
            pltpu.VMEM(density.shape, BF16),
            pltpu.VMEM(to_moments.shape, BF16),
            pltpu.VMEM(active.shape, jnp.int32),
            pltpu.VMEM(rates.shape, F32),
            pltpu.VMEM(lengths.shape, F32),
            pltpu.VMEM((32 * (clusters + 1) + 7, unknowns), F32),
            pltpu.VMEM((slabs, 1, lanes), F32),
            pltpu.SemaphoreType.DMA((11,)),
        ],
        compiler_params=pltpu.CompilerParams(vmem_limit_bytes=10 << 20),
        name="prep",
    )(*map(in_hbm, (density, active, to_moments, rates, lengths)))


def arrive_kernel(ends, far, decay, out):
    me = lax.axis_index("tm")
    slabs = ends.shape[0]
    steps, lanes = far.shape
    half = lanes // 2
    lane = lax.broadcasted_iota(jnp.int32, (1, lanes), 1)
    state = jnp.zeros((1, lanes), F32)
    for k in range(slabs):
        v = ends[k]
        swapped = pltpu.roll(v, half, 1)
        end = jnp.where(lane < half, v, swapped)
        factor = jnp.where(lane < half, swapped, v)
        state = jnp.where(k < me, factor * state + end, state)
    x = far[...] + decay[...] * state
    wide = lax.broadcasted_iota(jnp.int32, (steps // 2, lanes), 1)
    out[...] = jnp.where(wide < half, x[: steps // 2], x[steps // 2 :])


def arrive(ends, far, decay):
    steps, lanes = far.shape
    return pl.pallas_call(
        arrive_kernel,
        in_specs=[VMEM] * 3,
        out_specs=VMEM,
        out_shape=jax.ShapeDtypeStruct((steps // 2, lanes), F32),
        compiler_params=pltpu.CompilerParams(vmem_limit_bytes=4 << 20),
        cost_estimate=pl.CostEstimate(
            flops=10_000_000_000, bytes_accessed=1 << 20, transcendentals=0
        ),
        name="arrive",
    )(ends, far, decay)


def sum_kernel(a, b, out):
    out[...] = a[...] + b[...]


def summed(a, b):
    return pl.pallas_call(
        sum_kernel,
        in_specs=[VMEM] * 2,
        out_specs=VMEM,
        out_shape=jax.ShapeDtypeStruct(a.shape, F32),
        compiler_params=pltpu.CompilerParams(vmem_limit_bytes=1 << 20),
        name="summed",
    )(a, b)


def gathered(neighbours, window, cluster, rows):
    base = lax.axis_index("space") * neighbours.shape[1] - REACH
    return jnp.concatenate(
        [window[neighbours[j, cluster] - base, rows, :] for j in range(neighbours.shape[0])], axis=1
    )


def stacked(block):
    nb, unknowns, width = block.shape
    return block[...].reshape(nb * unknowns, width)


def near_of(neighbours, window, blocks, cluster):
    steps = window.shape[1]
    x = gathered(neighbours, window, cluster, pl.ds(0, steps))
    w = jnp.concatenate([stacked(block) for block in blocks], axis=1)
    both = jnp.dot(x, w, preferred_element_type=F32)
    now, later = jnp.split(both, 2, axis=1)
    return now + shifted_down(later, 1, 0.0), later[steps - 1 :]


def fetches_of(blocks, lags, groups, held, sems):
    waits, at = [], 0
    for k, (start, count) in enumerate(groups):
        waits.append(
            [
                pltpu.make_async_copy(
                    blocks.at[lag, pl.ds(start, count)],
                    held.at[n, pl.ds(at, count)],
                    sems.at[n, k],
                )
                for n, lag in enumerate(lags)
            ]
        )
        at += count
    return waits


def clusters_of(groups):
    return tuple(c for start, count in groups for c in range(start, start + count))


def near_groups(neighbours, window, groups, fetches, held, put):
    i = 0
    for (start, count), some in zip(groups, fetches):
        for fetch in some:
            fetch.wait()
        for cluster in range(start, start + count):
            blocks_here = [held.at[n, i] for n in range(held.shape[0])]
            put(i, cluster, *near_of(neighbours, window, blocks_here, cluster))
            i += 1


def inner_kernel(
    groups,
    later_groups,
    table,
    window,
    blocks,
    near,
    carry,
    neighbours,
    held,
    held_later,
    found,
    lines,
    sems,
    later_sems,
    out_sems,
):
    steps = window.shape[1]
    lags = blocks.shape[0]
    listed = pltpu.make_async_copy(table, neighbours, out_sems.at[0])
    listed.start()
    fetches = fetches_of(blocks, range(lags), groups, held, sems)
    later_fetches = fetches_of(blocks, (lags - 1,), later_groups, held_later, later_sems)
    for some in fetches + later_fetches:
        for fetch in some:
            fetch.start()
    listed.wait()

    def put(i, cluster, x, last):
        found[i] = x
        lines[cluster - REACH] = last

    near_groups(neighbours, window, groups, fetches, held, put)
    store = pltpu.make_async_copy(found, near, out_sems.at[1])
    store.start()
    i = 0
    for (start, count), some in zip(later_groups, later_fetches):
        for fetch in some:
            fetch.wait()
        for cluster in range(start, start + count):
            x = gathered(neighbours, window, cluster, pl.ds(steps - 16, 16))
            y = jnp.dot(x, stacked(held_later.at[0, i]), preferred_element_type=F32)
            lines[cluster - REACH] = y[15:]
            i += 1
    lines_store = pltpu.make_async_copy(lines, carry, out_sems.at[2])
    lines_store.start()
    store.wait()
    lines_store.wait()


def inner_near(neighbours, window, blocks, groups, later_groups):
    steps, unknowns = window.shape[1:]
    lags, clusters, nb = blocks.shape[:3]
    count, more = len(clusters_of(groups)), len(clusters_of(later_groups))
    block = (nb, unknowns, unknowns)
    return pl.pallas_call(
        functools.partial(inner_kernel, groups, later_groups),
        in_specs=[HBM, VMEM, HBM],
        out_specs=[HBM] * 2,
        out_shape=[
            pltpu.HBM((count, steps, unknowns), F32),
            pltpu.HBM((count + more, 1, unknowns), F32),
        ],
        scratch_shapes=[
            pltpu.SMEM(neighbours.shape, jnp.int32),
            pltpu.VMEM((lags, count, *block), BF16),
            pltpu.VMEM((1, more, *block), BF16),
            pltpu.VMEM((count, steps, unknowns), F32),
            pltpu.VMEM((count + more, 1, unknowns), F32),
            pltpu.SemaphoreType.DMA((lags, len(groups))),
            pltpu.SemaphoreType.DMA((1, len(later_groups))),
            pltpu.SemaphoreType.DMA((3,)),
        ],
        compiler_params=pltpu.CompilerParams(vmem_limit_bytes=16 << 20),
        name="inner",
    )(in_hbm(neighbours), window, in_hbm(blocks))


def edge_kernel(
    groups,
    table,
    window_in,
    from_pair,
    from_other,
    blocks,
    inner_carry,
    near,
    carry,
    window,
    neighbours,
    held,
    side_sems,
    sems,
):
    del window_in
    even = is_even()
    above = window.shape[0] - REACH

    def copy(src, dst, k):
        return pltpu.make_async_copy(src, dst, side_sems.at[k])

    sides = [
        copy(table, neighbours, 3),
        copy(from_pair, window.at[pl.ds(jnp.where(even, above, 0), REACH)], 0),
        copy(from_other, window.at[pl.ds(jnp.where(even, 0, above), REACH)], 1),
        copy(inner_carry, carry.at[pl.ds(REACH, inner_carry.shape[0])], 2),
    ]
    fetches = fetches_of(blocks, range(blocks.shape[0]), groups, held, sems)
    for c in sides:
        c.start()
    for some in fetches:
        for fetch in some:
            fetch.start()
    for c in sides:
        c.wait()

    def put(i, cluster, x, last):
        near[i] = x
        carry[cluster] = last

    near_groups(neighbours, window, groups, fetches, held, put)


def edge_near(neighbours, window, from_pair, from_other, blocks, inner_carry, groups):
    steps, unknowns = window.shape[1:]
    lags, clusters, nb = blocks.shape[:3]
    count = len(clusters_of(groups))
    return pl.pallas_call(
        functools.partial(edge_kernel, groups),
        in_specs=[HBM, VMEM, HBM, HBM, HBM, HBM],
        out_specs=[VMEM] * 3,
        out_shape=[
            jax.ShapeDtypeStruct((count, steps, unknowns), F32),
            jax.ShapeDtypeStruct((clusters, 1, unknowns), F32),
            jax.ShapeDtypeStruct(window.shape, BF16),
        ],
        scratch_shapes=[
            pltpu.SMEM(neighbours.shape, jnp.int32),
            pltpu.VMEM((lags, count, nb, unknowns, unknowns), BF16),
            pltpu.SemaphoreType.DMA((4,)),
            pltpu.SemaphoreType.DMA((lags, len(groups))),
        ],
        input_output_aliases={1: 2},
        compiler_params=pltpu.CompilerParams(vmem_limit_bytes=12 << 20),
        name="edge",
    )(
        in_hbm(neighbours),
        window,
        in_hbm(from_pair),
        in_hbm(from_other),
        in_hbm(blocks),
        in_hbm(inner_carry),
    )


def rest_kernel(
    groups, table, window, blocks, inner, from_moments, near, maps, neighbours, rows, held, side_sems, sems
):
    count = held.shape[1]
    sides = [
        pltpu.make_async_copy(table, neighbours, side_sems.at[0]),
        pltpu.make_async_copy(from_moments, rows, side_sems.at[1]),
        pltpu.make_async_copy(inner, near.at[pl.ds(count, inner.shape[0])], side_sems.at[2]),
    ]
    fetches = fetches_of(blocks, range(blocks.shape[0]), groups, held, sems)
    for c in sides[:2]:
        c.start()
    for some in fetches:
        for fetch in some:
            fetch.start()
    sides[2].start()
    sides[0].wait()
    sides[1].wait()
    w = jnp.transpose(rows[...], (1, 0, 2))
    for p in range(maps.shape[0]):
        x = jnp.concatenate([w[2 * p], w[2 * p + 1]], axis=1)
        maps[p] = jnp.concatenate([x, x], axis=0)

    def put(i, cluster, x, last):
        near[i] = x

    near_groups(neighbours, window, groups, fetches, held, put)
    sides[2].wait()


def rest_near(neighbours, window, blocks, inner, from_moments, groups):
    steps, unknowns = window.shape[1:]
    lags, clusters, nb = blocks.shape[:3]
    terms = from_moments.shape[0]
    count = len(clusters_of(groups))
    return pl.pallas_call(
        functools.partial(rest_kernel, groups),
        in_specs=[HBM, VMEM, HBM, HBM, HBM],
        out_specs=[VMEM] * 2,
        out_shape=[
            jax.ShapeDtypeStruct((count + inner.shape[0], steps, unknowns), F32),
            jax.ShapeDtypeStruct((clusters // 2, 2 * terms, 2 * unknowns), BF16),
        ],
        scratch_shapes=[
            pltpu.SMEM(neighbours.shape, jnp.int32),
            pltpu.VMEM(from_moments.shape, BF16),
            pltpu.VMEM((lags, count, nb, unknowns, unknowns), BF16),
            pltpu.SemaphoreType.DMA((3,)),
            pltpu.SemaphoreType.DMA((lags, len(groups))),
        ],
        compiler_params=pltpu.CompilerParams(vmem_limit_bytes=10 << 20),
        name="rest",
    )(in_hbm(neighbours), window, in_hbm(blocks), in_hbm(inner), in_hbm(from_moments))


def final_kernel(places, edge, rest, carry, *refs):
    parts = refs[:-6]
    maps, live, out, major, done, sems = refs[-6:]
    steps, clusters, unknowns = out.shape
    terms = maps.shape[1] // 2
    first = lax.axis_index("space") * clusters
    total = sum(part[...] for part in parts)
    lane = lax.broadcasted_iota(jnp.int32, total.shape, 1)
    size = steps // 2
    chunk = 32
    row = lax.broadcasted_iota(jnp.int32, (8, unknowns), 0)
    copies = []
    for half in range(2):
        mine = jnp.where(lane // terms == half, total, 0.0).astype(BF16)
        here = pl.ds(half * size, size)
        alive = live[here, :]
        for p in range(clusters // 2):
            both = jnp.dot(mine, maps[p], preferred_element_type=F32)
            for q in range(2):
                c = 2 * p + q
                which, at = places[c]
                near = (edge, rest)[which]
                x = both[:, q * unknowns : (q + 1) * unknowns] + near[at, here, :]
                if half == 0:
                    head = jnp.where(row == 0, jnp.broadcast_to(carry[c], row.shape), 0.0)
                    x = jnp.concatenate([x[:8] + head, x[8:]], axis=0)
                major[c] = jnp.where(alive > first + c, x, 0.0).astype(BF16)
        for i in range(size // chunk):
            start = half * size + i * chunk
            rows = pl.ds(start, chunk)
            done[rows] = jnp.transpose(major[:, pl.ds(i * chunk, chunk), :], (1, 0, 2))
            copies.append(
                pltpu.make_async_copy(done.at[rows], out.at[rows], sems.at[start // chunk])
            )
            copies[-1].start()
    for copy in copies:
        copy.wait()


def final(edge, rest, carry, parts, maps, live, orders):
    steps, unknowns = live.shape
    clusters = carry.shape[0]
    places = {c: (k, i) for k, order in enumerate(orders) for i, c in enumerate(order)}
    return pl.pallas_call(
        functools.partial(final_kernel, places),
        in_specs=[VMEM] * (5 + len(parts)),
        out_specs=HBM,
        out_shape=jax.ShapeDtypeStruct((steps, clusters, unknowns), BF16),
        scratch_shapes=[
            pltpu.VMEM((clusters, steps // 2, unknowns), BF16),
            pltpu.VMEM((steps, clusters, unknowns), BF16),
            pltpu.SemaphoreType.DMA((steps // 32,)),
        ],
        compiler_params=pltpu.CompilerParams(vmem_limit_bytes=10 << 20),
        name="final",
    )(edge, rest, carry, *parts, maps, live)


def exchanged(x, axis):
    return lax.all_to_all(x, axis, split_axis=0, concat_axis=0, tiled=True)


def across(x, axis, bit):
    count = lax.axis_size(axis)
    return lax.ppermute(x, axis, [(i, i ^ bit) for i in range(count)])


def swapped_from(x, axis, start):
    count = lax.axis_size(axis)
    route = []
    for i in range(start, count - 1, 2):
        route += [(i, i + 1), (i + 1, i)]
    return lax.ppermute(x, axis, route)


def passed_on(x, axis):
    count = lax.axis_size(axis)
    return lax.ppermute(x, axis, [(i, i + 1) for i in range(count - 1)])


def local(density, active, neighbours, near_blocks, to_moments, from_moments, decay_rates, lengths):
    steps = density.shape[0]
    slabs = lax.axis_size("tm")
    window, pair, other, far, decay, ends, live = prep(
        density,
        active.reshape(1, steps),
        to_moments,
        decay_rates.reshape(1, -1),
        lengths.reshape(1, steps),
        slabs,
    )
    ends = exchanged(ends, "tm")
    from_pair = swapped_from(pair, "space", 0)
    from_other = swapped_from(other, "space", 1)
    neighbours = neighbours.T
    clusters = density.shape[1]
    end = clusters - REACH
    full = ((12, 2), (14, 2), (16, 4))
    others = ((8, 4), (20, 4))
    sides = ((0, 2), (2, 2), (4, 4), (end, 4), (end + 4, 4))
    inner, inner_carry = inner_near(neighbours, window, near_blocks, full, others)
    ends, inner, inner_carry = lax.optimization_barrier((ends, inner, inner_carry))
    mine = arrive(ends, far, decay)
    mine = summed(mine, across(mine, "space", 1))
    theirs = across(mine, "space", 2)
    inner_carry, mine = lax.optimization_barrier((inner_carry, mine))
    edge, carry, window = edge_near(
        neighbours, window, from_pair, from_other, near_blocks, inner_carry, sides
    )
    theirs, carry = lax.optimization_barrier((theirs, carry))
    mine = summed(mine, theirs)
    theirs = across(mine, "space", 4)
    carry = passed_on(carry, "tm")
    inner, mine = lax.optimization_barrier((inner, mine))
    rest, maps = rest_near(neighbours, window, near_blocks, inner, from_moments, others)
    orders = (clusters_of(sides), clusters_of(others + full))
    return final(edge, rest, carry, (mine, theirs), maps, live, orders)


def solution(mesh):
    placed = (
        P("tm", "space", None),
        P("tm"),
        P("space", None),
        P(None, "space", None, None, None),
        P(None, "space", None),
        P(None, "space", None),
        P(),
        P("tm"),
    )
    return jax.shard_map(
        local, mesh=mesh, in_specs=placed, out_specs=P("tm", "space", None), check_vma=False
    )
```

```python
import functools

import jax
import jax.numpy as jnp
from jax import lax
from jax.experimental import pallas as pl
from jax.experimental.pallas import tpu as pltpu
from jax.sharding import PartitionSpec as P

REACH = 8
F32 = jnp.float32
BF16 = jnp.bfloat16
HBM = pl.BlockSpec(memory_space=pltpu.HBM)
VMEM = pl.BlockSpec(memory_space=pltpu.VMEM)


def in_hbm(x):
    return pltpu.with_memory_space_constraint(x, pltpu.HBM)


def in_vmem(x):
    return pltpu.with_memory_space_constraint(x, pltpu.VMEM)


def column(row, lanes):
    return jnp.transpose(jnp.broadcast_to(row, (lanes, row.shape[1])))


def shifted_down(v, steps, fill):
    rows = v.shape[0]
    if steps < 8:
        moved = pltpu.roll(v, steps, 0)
        at = lax.broadcasted_iota(jnp.int32, v.shape, 0)
        return jnp.where(at < steps, jnp.full_like(v, fill), moved)
    return jnp.concatenate([jnp.full((steps, v.shape[1]), fill, v.dtype), v[: rows - steps]], 0)


def doubled(row):
    return jnp.concatenate([row, row], axis=1)


def is_even():
    return lax.rem(lax.axis_index("space"), 2) == 0


def prep_kernel(
    density,
    active,
    to_moments,
    rates,
    lengths,
    window,
    pair,
    other,
    far,
    decay,
    ends,
    live,
    dense,
    maps,
    active_row,
    rates_row,
    lengths_row,
    flat,
    lines,
    sems,
):
    steps, clusters, unknowns = density.shape
    terms = to_moments.shape[0]
    pieces = 4
    size = steps // pieces
    chunk = 32
    pitch = clusters + 1
    first = lax.axis_index("space") * clusters

    def copy(src, dst, k):
        return pltpu.make_async_copy(src, dst, sems.at[k])

    small = [
        copy(active, active_row, 0),
        copy(lengths, lengths_row, 1),
        copy(rates, rates_row, 2),
    ]
    parts = [
        copy(density.at[pl.ds(k * size, size)], dense.at[pl.ds(k * size, size)], 4 + k)
        for k in range(pieces)
    ]
    weights = copy(to_moments, maps, 3)
    for c in small + parts + [weights]:
        c.start()
    for c in small:
        c.wait()
    live[...] = column(active_row[...], unknowns)

    for k in range(pieces):
        parts[k].wait()

        def spread(i, _):
            start = pl.multiple_of(k * size + i * chunk, chunk)
            here = pl.ds(start, chunk)
            x = dense[here].astype(F32)
            for t in range(chunk):
                flat[pl.ds(t * pitch, clusters), :] = x[t]
            alive = live[here, :]
            for c in range(clusters):
                y = flat[pl.ds(c, chunk, stride=pitch), :]
                y = jnp.where(alive > first + c, y, 0.0)
                window[REACH + c, here, :] = y.astype(BF16)
            return 0

        lax.fori_loop(0, size // chunk, spread, 0)

    even = is_even()
    above = clusters
    sides = [
        copy(window.at[pl.ds(jnp.where(even, above, REACH), REACH)], pair, 8),
        copy(window.at[pl.ds(jnp.where(even, REACH, above), REACH)], other, 9),
    ]
    for c in sides:
        c.start()

    weights.wait()
    w = jnp.transpose(maps[...], (1, 0, 2))
    total = jnp.zeros((steps, 2 * terms), F32)
    for c in range(0, clusters, 2):
        x = jnp.concatenate([window[REACH + c], window[REACH + c + 1]], axis=1)
        y = jnp.concatenate([w[c], w[c + 1]], axis=1)
        y = jnp.concatenate([y, y], axis=0)
        total = total + lax.dot_general(
            x, y, (((1,), (1,)), ((), ())), preferred_element_type=F32
        )
    d = jnp.exp(-doubled(rates_row[...]) * column(lengths_row[...], 2 * terms))
    s = 1
    while s < steps:
        before = shifted_down(total, s, 0.0)
        factor = shifted_down(d, s, 1.0)
        total = total + d * before
        d = d * factor
        s *= 2
    lane = lax.broadcasted_iota(jnp.int32, (1, 2 * terms), 1)
    line = jnp.where(lane < terms, total[steps - 1 :], d[steps - 1 :])
    for k in range(ends.shape[0]):
        lines[k] = line
    sides.append(copy(lines, ends, 10))
    sides[-1].start()
    scale = jnp.sqrt(2.0 * doubled(rates_row[...]))
    far[...] = shifted_down(total, 1, 0.0) * scale
    decay[...] = shifted_down(d, 1, 1.0) * scale
    for c in sides:
        c.wait()


def prep(density, active, to_moments, rates, lengths, slabs):
    steps, clusters, unknowns = density.shape
    terms = to_moments.shape[0]
    lanes = 2 * terms
    side = pltpu.HBM((REACH, steps, unknowns), BF16)
    return pl.pallas_call(
        prep_kernel,
        in_specs=[HBM] * 5,
        out_specs=[VMEM, HBM, HBM, VMEM, VMEM, HBM, VMEM],
        out_shape=[
            jax.ShapeDtypeStruct((clusters + 2 * REACH, steps, unknowns), BF16),
            side,
            side,
            jax.ShapeDtypeStruct((steps, lanes), F32),
            jax.ShapeDtypeStruct((steps, lanes), F32),
            pltpu.HBM((slabs, 1, lanes), F32),
            jax.ShapeDtypeStruct((steps, unknowns), jnp.int32),
        ],
        scratch_shapes=[
            pltpu.VMEM(density.shape, BF16),
            pltpu.VMEM(to_moments.shape, BF16),
            pltpu.VMEM(active.shape, jnp.int32),
            pltpu.VMEM(rates.shape, F32),
            pltpu.VMEM(lengths.shape, F32),
            pltpu.VMEM((32 * (clusters + 1) + 7, unknowns), F32),
            pltpu.VMEM((slabs, 1, lanes), F32),
            pltpu.SemaphoreType.DMA((11,)),
        ],
        compiler_params=pltpu.CompilerParams(vmem_limit_bytes=10 << 20),
        name="prep",
    )(*map(in_hbm, (density, active, to_moments, rates, lengths)))


def arrive_kernel(ends, far, decay, out):
    me = lax.axis_index("tm")
    slabs = ends.shape[0]
    steps, lanes = far.shape
    half = lanes // 2
    lane = lax.broadcasted_iota(jnp.int32, (1, lanes), 1)
    state = jnp.zeros((1, lanes), F32)
    for k in range(slabs):
        v = ends[k]
        swapped = pltpu.roll(v, half, 1)
        end = jnp.where(lane < half, v, swapped)
        factor = jnp.where(lane < half, swapped, v)
        state = jnp.where(k < me, factor * state + end, state)
    x = far[...] + decay[...] * state
    wide = lax.broadcasted_iota(jnp.int32, (steps // 2, lanes), 1)
    out[...] = jnp.where(wide < half, x[: steps // 2], x[steps // 2 :])


def arrive(ends, far, decay):
    steps, lanes = far.shape
    return pl.pallas_call(
        arrive_kernel,
        in_specs=[VMEM] * 3,
        out_specs=VMEM,
        out_shape=jax.ShapeDtypeStruct((steps // 2, lanes), F32),
        compiler_params=pltpu.CompilerParams(vmem_limit_bytes=4 << 20),
        cost_estimate=pl.CostEstimate(
            flops=10_000_000_000, bytes_accessed=1 << 20, transcendentals=0
        ),
        name="arrive",
    )(ends, far, decay)


def pair_kernel(a, b, out):
    out[...] = (a[...] + b[...]).astype(BF16)


def pair_sum(a, b):
    return pl.pallas_call(
        pair_kernel,
        in_specs=[VMEM] * 2,
        out_specs=VMEM,
        out_shape=jax.ShapeDtypeStruct(a.shape, BF16),
        compiler_params=pltpu.CompilerParams(vmem_limit_bytes=4 << 20),
        name="pair_sum",
    )(a, b)


def gathered(neighbours, window, cluster, rows):
    base = lax.axis_index("space") * neighbours.shape[1] - REACH
    return jnp.concatenate(
        [window[neighbours[j, cluster] - base, rows, :] for j in range(neighbours.shape[0])], axis=1
    )


def stacked(block):
    nb, unknowns, width = block.shape
    return block[...].reshape(nb * unknowns, width)


def near_of(neighbours, window, blocks, cluster):
    steps = window.shape[1]
    x = gathered(neighbours, window, cluster, pl.ds(0, steps))
    w = jnp.concatenate([stacked(block) for block in blocks], axis=1)
    both = jnp.dot(x, w, preferred_element_type=F32)
    now, later = jnp.split(both, 2, axis=1)
    return now + shifted_down(later, 1, 0.0), later[steps - 1 :]


def ends_kernel(starts, table, window, blocks, carry, neighbours, held, lines, sems):
    steps = window.shape[1]
    lags = blocks.shape[0]
    count = held.shape[0] // len(starts)
    listed = pltpu.make_async_copy(table, neighbours, sems.at[0])
    listed.start()
    fetches = [
        pltpu.make_async_copy(
            blocks.at[lags - 1, pl.ds(start, count)],
            held.at[pl.ds(k * count, count)],
            sems.at[1 + k],
        )
        for k, start in enumerate(starts)
    ]
    for fetch in fetches:
        fetch.start()
    listed.wait()
    for k, start in enumerate(starts):
        fetches[k].wait()
        for i in range(count):
            x = gathered(neighbours, window, start + i, pl.ds(steps - 16, 16))
            w = stacked(held.at[k * count + i])
            lines[k * count + i] = jnp.dot(x, w, preferred_element_type=F32)[15:]
    store = pltpu.make_async_copy(lines, carry, sems.at[1 + len(starts)])
    store.start()
    store.wait()


def ends_near(neighbours, window, blocks, starts, count):
    unknowns = window.shape[2]
    nb = blocks.shape[2]
    more = len(starts) * count
    return pl.pallas_call(
        functools.partial(ends_kernel, starts),
        in_specs=[HBM, VMEM, HBM],
        out_specs=HBM,
        out_shape=pltpu.HBM((more, 1, unknowns), F32),
        scratch_shapes=[
            pltpu.SMEM(neighbours.shape, jnp.int32),
            pltpu.VMEM((more, nb, unknowns, unknowns), BF16),
            pltpu.VMEM((more, 1, unknowns), F32),
            pltpu.SemaphoreType.DMA((2 + len(starts),)),
        ],
        compiler_params=pltpu.CompilerParams(vmem_limit_bytes=4 << 20),
        name="ends",
    )(in_hbm(neighbours), window, in_hbm(blocks))


def edge_kernel(
    order,
    starts,
    table,
    window_in,
    from_pair,
    from_other,
    blocks,
    inner_carry,
    near,
    carry,
    window,
    neighbours,
    sems,
):
    del window_in
    even = is_even()
    above = window.shape[0] - REACH

    def copy(src, dst, k):
        return pltpu.make_async_copy(src, dst, sems.at[k])

    count = inner_carry.shape[0] // len(starts)
    listed = copy(table, neighbours, 0)
    sides = [
        copy(from_pair, window.at[pl.ds(jnp.where(even, above, 0), REACH)], 1),
        copy(from_other, window.at[pl.ds(jnp.where(even, 0, above), REACH)], 2),
    ]
    rows = [
        copy(inner_carry.at[pl.ds(k * count, count)], carry.at[pl.ds(start, count)], 3 + k)
        for k, start in enumerate(starts)
    ]
    listed.start()
    for c in sides + rows:
        c.start()
    listed.wait()
    for i, cluster in enumerate(order):
        if i == REACH:
            for c in sides:
                c.wait()
        blocks_here = [blocks.at[lag, cluster] for lag in range(blocks.shape[0])]
        near[i], carry[cluster] = near_of(neighbours, window, blocks_here, cluster)
    for c in rows:
        c.wait()


def edge_near(neighbours, window, from_pair, from_other, blocks, inner_carry, order, starts):
    steps, unknowns = window.shape[1:]
    clusters = blocks.shape[1]
    return pl.pallas_call(
        functools.partial(edge_kernel, order, starts),
        in_specs=[HBM, VMEM, HBM, HBM, VMEM, HBM],
        out_specs=[VMEM] * 3,
        out_shape=[
            jax.ShapeDtypeStruct((len(order), steps, unknowns), F32),
            jax.ShapeDtypeStruct((clusters, 1, unknowns), F32),
            jax.ShapeDtypeStruct(window.shape, BF16),
        ],
        scratch_shapes=[
            pltpu.SMEM(neighbours.shape, jnp.int32),
            pltpu.SemaphoreType.DMA((3 + len(starts),)),
        ],
        input_output_aliases={1: 2},
        compiler_params=pltpu.CompilerParams(vmem_limit_bytes=8 << 20),
        name="edge",
    )(
        in_hbm(neighbours),
        window,
        in_hbm(from_pair),
        in_hbm(from_other),
        in_vmem(blocks),
        in_hbm(inner_carry),
    )


def rest_kernel(order, table, window, blocks, from_moments, near, maps, neighbours, rows, sems):
    listed = pltpu.make_async_copy(table, neighbours, sems.at[0])
    fetch = pltpu.make_async_copy(from_moments, rows, sems.at[1])
    listed.start()
    fetch.start()
    listed.wait()
    for i, cluster in enumerate(order):
        blocks_here = [blocks.at[lag, cluster] for lag in range(blocks.shape[0])]
        near[i], _ = near_of(neighbours, window, blocks_here, cluster)
    fetch.wait()
    w = jnp.transpose(rows[...], (1, 0, 2))
    for p in range(maps.shape[0]):
        x = jnp.concatenate([w[2 * p], w[2 * p + 1]], axis=1)
        maps[p] = jnp.concatenate([x, x], axis=0)


def rest_near(neighbours, window, blocks, from_moments, order):
    steps, unknowns = window.shape[1:]
    clusters = blocks.shape[1]
    terms = from_moments.shape[0]
    return pl.pallas_call(
        functools.partial(rest_kernel, order),
        in_specs=[HBM, VMEM, VMEM, HBM],
        out_specs=[VMEM] * 2,
        out_shape=[
            jax.ShapeDtypeStruct((len(order), steps, unknowns), F32),
            jax.ShapeDtypeStruct((clusters // 2, 2 * terms, 2 * unknowns), BF16),
        ],
        scratch_shapes=[
            pltpu.SMEM(neighbours.shape, jnp.int32),
            pltpu.VMEM(from_moments.shape, BF16),
            pltpu.SemaphoreType.DMA((2,)),
        ],
        compiler_params=pltpu.CompilerParams(vmem_limit_bytes=8 << 20),
        name="rest",
    )(in_hbm(neighbours), window, in_vmem(blocks), in_hbm(from_moments))


def final_kernel(places, edge, rest, carry, *refs):
    parts = refs[:4]
    maps, live, out, major, done, sems = refs[4:]
    steps, clusters, unknowns = out.shape
    terms = maps.shape[1] // 2
    first = lax.axis_index("space") * clusters
    total = parts[0][...].astype(F32)
    for part in parts[1:]:
        total = total + part[...].astype(F32)
    lane = lax.broadcasted_iota(jnp.int32, total.shape, 1)
    size = steps // 2
    chunk = 32
    row = lax.broadcasted_iota(jnp.int32, (8, unknowns), 0)
    copies = []
    for half in range(2):
        mine = jnp.where(lane // terms == half, total, 0.0).astype(BF16)
        here = pl.ds(half * size, size)
        alive = live[here, :]
        for p in range(clusters // 2):
            both = jnp.dot(mine, maps[p], preferred_element_type=F32)
            for q in range(2):
                c = 2 * p + q
                which, at = places[c]
                near = (edge, rest)[which]
                x = both[:, q * unknowns : (q + 1) * unknowns] + near[at, here, :]
                if half == 0:
                    head = jnp.where(row == 0, jnp.broadcast_to(carry[c], row.shape), 0.0)
                    x = jnp.concatenate([x[:8] + head, x[8:]], axis=0)
                major[c] = jnp.where(alive > first + c, x, 0.0).astype(BF16)
        for i in range(size // chunk):
            start = half * size + i * chunk
            rows = pl.ds(start, chunk)
            done[rows] = jnp.transpose(major[:, pl.ds(i * chunk, chunk), :], (1, 0, 2))
            copies.append(
                pltpu.make_async_copy(done.at[rows], out.at[rows], sems.at[start // chunk])
            )
            copies[-1].start()
    for copy in copies:
        copy.wait()


def final(edge, rest, carry, parts, maps, live, orders):
    steps, unknowns = live.shape
    clusters = carry.shape[0]
    places = {c: (k, i) for k, order in enumerate(orders) for i, c in enumerate(order)}
    return pl.pallas_call(
        functools.partial(final_kernel, places),
        in_specs=[VMEM] * (5 + len(parts)),
        out_specs=HBM,
        out_shape=jax.ShapeDtypeStruct((steps, clusters, unknowns), BF16),
        scratch_shapes=[
            pltpu.VMEM((clusters, steps // 2, unknowns), BF16),
            pltpu.VMEM((steps, clusters, unknowns), BF16),
            pltpu.SemaphoreType.DMA((steps // 32,)),
        ],
        compiler_params=pltpu.CompilerParams(vmem_limit_bytes=10 << 20),
        name="final",
    )(edge, rest, carry, *parts, maps, live)


def exchanged(x, axis):
    return lax.all_to_all(x, axis, split_axis=0, concat_axis=0, tiled=True)


def swapped_from(x, axis, start):
    count = lax.axis_size(axis)
    route = []
    for i in range(start, count - 1, 2):
        route += [(i, i + 1), (i + 1, i)]
    return lax.ppermute(x, axis, route)


def from_chip(x, axis, distance):
    count = lax.axis_size(axis)
    return lax.ppermute(x, axis, [(i, (i + 2 * distance) % count) for i in range(count)])


def passed_on(x, axis):
    count = lax.axis_size(axis)
    return lax.ppermute(x, axis, [(i, i + 1) for i in range(count - 1)])


def local(density, active, neighbours, near_blocks, to_moments, from_moments, decay_rates, lengths):
    steps = density.shape[0]
    slabs, chips = lax.axis_size("tm"), lax.axis_size("space") // 2
    window, pair, other, far, decay, ends, live = prep(
        density,
        active.reshape(1, steps),
        to_moments,
        decay_rates.reshape(1, -1),
        lengths.reshape(1, steps),
        slabs,
    )
    ends = exchanged(ends, "tm")
    from_pair = swapped_from(pair, "space", 0)
    from_other = swapped_from(other, "space", 1)
    neighbours = neighbours.T
    clusters = density.shape[1]
    half = REACH // 2
    starts = (REACH, clusters - REACH - half)
    later = tuple(c for start in starts for c in range(start, start + half))
    sides = tuple(range(REACH)) + tuple(range(clusters - REACH, clusters))
    early = tuple(c for c in range(clusters) if c not in later + sides) + sides
    inner_carry = ends_near(neighbours, window, near_blocks, starts, half)
    ends, inner_carry = lax.optimization_barrier((ends, inner_carry))
    mine = arrive(ends, far, decay)
    mine = pair_sum(mine, swapped_from(mine, "space", 0))
    parts = [mine] + [from_chip(mine, "space", d) for d in range(1, chips)]
    inner_carry, mine = lax.optimization_barrier((inner_carry, mine))
    edge, carry, window = edge_near(
        neighbours, window, from_pair, from_other, near_blocks, inner_carry, early, starts
    )
    carry = passed_on(carry, "tm")
    rest, maps = rest_near(neighbours, window, near_blocks, from_moments, later)
    return final(edge, rest, carry, parts, maps, live, (early, later))


def solution(mesh):
    placed = (
        P("tm", "space", None),
        P("tm"),
        P("space", None),
        P(None, "space", None, None, None),
        P(None, "space", None),
        P(None, "space", None),
        P(),
        P("tm"),
    )
    return jax.shard_map(
        local, mesh=mesh, in_specs=placed, out_specs=P("tm", "space", None), check_vma=False
    )
```

```python
import functools

import jax
import jax.numpy as jnp
from jax import lax
from jax.experimental import pallas as pl
from jax.experimental.pallas import tpu as pltpu
from jax.sharding import PartitionSpec as P

REACH = 8
F32 = jnp.float32
BF16 = jnp.bfloat16
HBM = pl.BlockSpec(memory_space=pltpu.HBM)
VMEM = pl.BlockSpec(memory_space=pltpu.VMEM)


def in_hbm(x):
    return pltpu.with_memory_space_constraint(x, pltpu.HBM)


def in_vmem(x):
    return pltpu.with_memory_space_constraint(x, pltpu.VMEM)


def column(row, lanes):
    return jnp.transpose(jnp.broadcast_to(row, (lanes, row.shape[1])))


def shifted_down(v, steps, fill):
    rows = v.shape[0]
    if steps < 8:
        moved = pltpu.roll(v, steps, 0)
        at = lax.broadcasted_iota(jnp.int32, v.shape, 0)
        return jnp.where(at < steps, jnp.full_like(v, fill), moved)
    return jnp.concatenate([jnp.full((steps, v.shape[1]), fill, v.dtype), v[: rows - steps]], 0)


def doubled(row):
    return jnp.concatenate([row, row], axis=1)


def is_even():
    return lax.rem(lax.axis_index("space"), 2) == 0


def prep_kernel(
    density,
    active,
    to_moments,
    rates,
    lengths,
    window,
    pair,
    other,
    far,
    decay,
    ends,
    live,
    dense,
    maps,
    active_row,
    rates_row,
    lengths_row,
    flat,
    lines,
    sems,
):
    steps, clusters, unknowns = density.shape
    terms = to_moments.shape[0]
    pieces = 4
    size = steps // pieces
    chunk = 32
    pitch = clusters + 1
    first = lax.axis_index("space") * clusters

    def copy(src, dst, k):
        return pltpu.make_async_copy(src, dst, sems.at[k])

    small = [
        copy(active, active_row, 0),
        copy(lengths, lengths_row, 1),
        copy(rates, rates_row, 2),
    ]
    parts = [
        copy(density.at[pl.ds(k * size, size)], dense.at[pl.ds(k * size, size)], 4 + k)
        for k in range(pieces)
    ]
    weights = copy(to_moments, maps, 3)
    for c in small + parts + [weights]:
        c.start()
    for c in small:
        c.wait()
    live[...] = column(active_row[...], unknowns)

    for k in range(pieces):
        parts[k].wait()

        def spread(i, _):
            start = pl.multiple_of(k * size + i * chunk, chunk)
            here = pl.ds(start, chunk)
            x = dense[here].astype(F32)
            for t in range(chunk):
                flat[pl.ds(t * pitch, clusters), :] = x[t]
            alive = live[here, :]
            for c in range(clusters):
                y = flat[pl.ds(c, chunk, stride=pitch), :]
                y = jnp.where(alive > first + c, y, 0.0)
                window[REACH + c, here, :] = y.astype(BF16)
            return 0

        lax.fori_loop(0, size // chunk, spread, 0)

    even = is_even()
    above = clusters
    sides = [
        copy(window.at[pl.ds(jnp.where(even, above, REACH), REACH)], pair, 8),
        copy(window.at[pl.ds(jnp.where(even, REACH, above), REACH)], other, 9),
    ]
    for c in sides:
        c.start()

    weights.wait()
    w = jnp.transpose(maps[...], (1, 0, 2))
    total = jnp.zeros((steps, 2 * terms), F32)
    for c in range(0, clusters, 2):
        x = jnp.concatenate([window[REACH + c], window[REACH + c + 1]], axis=1)
        y = jnp.concatenate([w[c], w[c + 1]], axis=1)
        y = jnp.concatenate([y, y], axis=0)
        total = total + lax.dot_general(
            x, y, (((1,), (1,)), ((), ())), preferred_element_type=F32
        )
    d = jnp.exp(-doubled(rates_row[...]) * column(lengths_row[...], 2 * terms))
    s = 1
    while s < steps:
        before = shifted_down(total, s, 0.0)
        factor = shifted_down(d, s, 1.0)
        total = total + d * before
        d = d * factor
        s *= 2
    lane = lax.broadcasted_iota(jnp.int32, (1, 2 * terms), 1)
    line = jnp.where(lane < terms, total[steps - 1 :], d[steps - 1 :])
    for k in range(ends.shape[0]):
        lines[k] = line
    sides.append(copy(lines, ends, 10))
    sides[-1].start()
    scale = jnp.sqrt(2.0 * doubled(rates_row[...]))
    far[...] = shifted_down(total, 1, 0.0) * scale
    decay[...] = shifted_down(d, 1, 1.0) * scale
    for c in sides:
        c.wait()


def prep(density, active, to_moments, rates, lengths, slabs):
    steps, clusters, unknowns = density.shape
    terms = to_moments.shape[0]
    lanes = 2 * terms
    side = pltpu.HBM((REACH, steps, unknowns), BF16)
    return pl.pallas_call(
        prep_kernel,
        in_specs=[HBM] * 5,
        out_specs=[VMEM, HBM, HBM, VMEM, VMEM, HBM, VMEM],
        out_shape=[
            jax.ShapeDtypeStruct((clusters + 2 * REACH, steps, unknowns), BF16),
            side,
            side,
            jax.ShapeDtypeStruct((steps, lanes), F32),
            jax.ShapeDtypeStruct((steps, lanes), F32),
            pltpu.HBM((slabs, 1, lanes), F32),
            jax.ShapeDtypeStruct((steps, unknowns), jnp.int32),
        ],
        scratch_shapes=[
            pltpu.VMEM(density.shape, BF16),
            pltpu.VMEM(to_moments.shape, BF16),
            pltpu.VMEM(active.shape, jnp.int32),
            pltpu.VMEM(rates.shape, F32),
            pltpu.VMEM(lengths.shape, F32),
            pltpu.VMEM((32 * (clusters + 1) + 7, unknowns), F32),
            pltpu.VMEM((slabs, 1, lanes), F32),
            pltpu.SemaphoreType.DMA((11,)),
        ],
        compiler_params=pltpu.CompilerParams(vmem_limit_bytes=10 << 20),
        name="prep",
    )(*map(in_hbm, (density, active, to_moments, rates, lengths)))


def arrive_kernel(ends, far, decay, out):
    me = lax.axis_index("tm")
    slabs = ends.shape[0]
    steps, lanes = far.shape
    half = lanes // 2
    lane = lax.broadcasted_iota(jnp.int32, (1, lanes), 1)
    state = jnp.zeros((1, lanes), F32)
    for k in range(slabs):
        v = ends[k]
        swapped = pltpu.roll(v, half, 1)
        end = jnp.where(lane < half, v, swapped)
        factor = jnp.where(lane < half, swapped, v)
        state = jnp.where(k < me, factor * state + end, state)
    x = far[...] + decay[...] * state
    wide = lax.broadcasted_iota(jnp.int32, (steps // 2, lanes), 1)
    out[...] = jnp.where(wide < half, x[: steps // 2], x[steps // 2 :])


def arrive(ends, far, decay):
    steps, lanes = far.shape
    return pl.pallas_call(
        arrive_kernel,
        in_specs=[VMEM] * 3,
        out_specs=VMEM,
        out_shape=jax.ShapeDtypeStruct((steps // 2, lanes), F32),
        compiler_params=pltpu.CompilerParams(vmem_limit_bytes=4 << 20),
        cost_estimate=pl.CostEstimate(
            flops=10_000_000_000, bytes_accessed=1 << 20, transcendentals=0
        ),
        name="arrive",
    )(ends, far, decay)


def pair_kernel(a, b, out):
    out[...] = (a[...] + b[...]).astype(BF16)


def pair_sum(a, b):
    return pl.pallas_call(
        pair_kernel,
        in_specs=[VMEM] * 2,
        out_specs=VMEM,
        out_shape=jax.ShapeDtypeStruct(a.shape, BF16),
        compiler_params=pltpu.CompilerParams(vmem_limit_bytes=4 << 20),
        name="pair_sum",
    )(a, b)


def gathered(neighbours, window, cluster, rows):
    base = lax.axis_index("space") * neighbours.shape[1] - REACH
    return jnp.concatenate(
        [window[neighbours[j, cluster] - base, rows, :] for j in range(neighbours.shape[0])], axis=1
    )


def stacked(block):
    nb, unknowns, width = block.shape
    return block[...].reshape(nb * unknowns, width)


def near_of(neighbours, window, blocks, cluster):
    steps = window.shape[1]
    x = gathered(neighbours, window, cluster, pl.ds(0, steps))
    w = jnp.concatenate([stacked(block) for block in blocks], axis=1)
    both = jnp.dot(x, w, preferred_element_type=F32)
    now, later = jnp.split(both, 2, axis=1)
    return now + shifted_down(later, 1, 0.0), later[steps - 1 :]


def fetches_of(blocks, lags, groups, held, sems):
    waits, at = [], 0
    for k, (start, count) in enumerate(groups):
        waits.append(
            [
                pltpu.make_async_copy(
                    blocks.at[lag, pl.ds(start, count)],
                    held.at[n, pl.ds(at, count)],
                    sems.at[n, k],
                )
                for n, lag in enumerate(lags)
            ]
        )
        at += count
    return waits


def clusters_of(groups):
    return tuple(c for start, count in groups for c in range(start, start + count))


def near_groups(neighbours, window, groups, fetches, held, put):
    i = 0
    for (start, count), some in zip(groups, fetches):
        for fetch in some:
            fetch.wait()
        for cluster in range(start, start + count):
            blocks_here = [held.at[n, i] for n in range(held.shape[0])]
            put(i, cluster, *near_of(neighbours, window, blocks_here, cluster))
            i += 1


def inner_kernel(
    groups,
    later_groups,
    table,
    window,
    blocks,
    near,
    carry,
    neighbours,
    held,
    held_later,
    found,
    lines,
    sems,
    later_sems,
    out_sems,
):
    lags = blocks.shape[0]
    listed = pltpu.make_async_copy(table, neighbours, out_sems.at[0])
    listed.start()
    fetches = fetches_of(blocks, range(lags), groups, held, sems)
    later_fetches = fetches_of(blocks, (lags - 1,), later_groups, held_later, later_sems)
    for some in fetches + later_fetches:
        for fetch in some:
            fetch.start()
    listed.wait()

    def put(i, cluster, x, last):
        found[i] = x
        lines[cluster - REACH] = last

    near_groups(neighbours, window, groups, fetches, held, put)
    store = pltpu.make_async_copy(found, near, out_sems.at[1])
    store.start()
    i = 0
    for (start, count), some in zip(later_groups, later_fetches):
        for fetch in some:
            fetch.wait()
        for cluster in range(start, start + count):
            lines[cluster - REACH] = last_row(neighbours, window, held_later.at[0, i], cluster)
            i += 1
    lines_store = pltpu.make_async_copy(lines, carry, out_sems.at[2])
    lines_store.start()
    store.wait()
    lines_store.wait()


def inner_near(neighbours, window, blocks, groups, later_groups):
    steps, unknowns = window.shape[1:]
    lags, clusters, nb = blocks.shape[:3]
    count, more = len(clusters_of(groups)), len(clusters_of(later_groups))
    block = (nb, unknowns, unknowns)
    return pl.pallas_call(
        functools.partial(inner_kernel, groups, later_groups),
        in_specs=[HBM, VMEM, HBM],
        out_specs=[HBM] * 2,
        out_shape=[
            pltpu.HBM((count, steps, unknowns), F32),
            pltpu.HBM((count + more, 1, unknowns), F32),
        ],
        scratch_shapes=[
            pltpu.SMEM(neighbours.shape, jnp.int32),
            pltpu.VMEM((lags, count, *block), BF16),
            pltpu.VMEM((1, more, *block), BF16),
            pltpu.VMEM((count, steps, unknowns), F32),
            pltpu.VMEM((count + more, 1, unknowns), F32),
            pltpu.SemaphoreType.DMA((lags, len(groups))),
            pltpu.SemaphoreType.DMA((1, len(later_groups))),
            pltpu.SemaphoreType.DMA((3,)),
        ],
        compiler_params=pltpu.CompilerParams(vmem_limit_bytes=16 << 20),
        name="inner",
    )(in_hbm(neighbours), window, in_hbm(blocks))


def last_row(neighbours, window, block, cluster):
    steps = window.shape[1]
    x = gathered(neighbours, window, cluster, pl.ds(steps - 16, 16))
    return jnp.dot(x, stacked(block), preferred_element_type=F32)[15:]


def edge_kernel(
    order,
    ends_only,
    table,
    window_in,
    from_pair,
    from_other,
    blocks,
    inner_carry,
    near,
    carry,
    window,
    neighbours,
    sems,
):
    del window_in
    even = is_even()
    above = window.shape[0] - REACH
    lags = blocks.shape[0]

    def copy(src, dst, k):
        return pltpu.make_async_copy(src, dst, sems.at[k])

    sides = [
        copy(table, neighbours, 0),
        copy(from_pair, window.at[pl.ds(jnp.where(even, above, 0), REACH)], 1),
        copy(from_other, window.at[pl.ds(jnp.where(even, 0, above), REACH)], 2),
        copy(inner_carry, carry.at[pl.ds(REACH, inner_carry.shape[0])], 3),
    ]
    for c in sides:
        c.start()
    for c in sides:
        c.wait()
    for i, cluster in enumerate(order):
        blocks_here = [blocks.at[lag, cluster] for lag in range(lags)]
        near[i], carry[cluster] = near_of(neighbours, window, blocks_here, cluster)
    for cluster in ends_only:
        carry[cluster] = last_row(neighbours, window, blocks.at[lags - 1, cluster], cluster)


def edge_near(
    neighbours, window, from_pair, from_other, blocks, inner_carry, order, ends_only
):
    steps, unknowns = window.shape[1:]
    clusters = blocks.shape[1]
    return pl.pallas_call(
        functools.partial(edge_kernel, order, ends_only),
        in_specs=[HBM, VMEM, HBM, HBM, VMEM, HBM],
        out_specs=[VMEM] * 3,
        out_shape=[
            jax.ShapeDtypeStruct((len(order), steps, unknowns), F32),
            jax.ShapeDtypeStruct((clusters, 1, unknowns), F32),
            jax.ShapeDtypeStruct(window.shape, BF16),
        ],
        scratch_shapes=[
            pltpu.SMEM(neighbours.shape, jnp.int32),
            pltpu.SemaphoreType.DMA((4,)),
        ],
        input_output_aliases={1: 2},
        compiler_params=pltpu.CompilerParams(vmem_limit_bytes=8 << 20),
        name="edge",
    )(
        in_hbm(neighbours),
        window,
        in_hbm(from_pair),
        in_hbm(from_other),
        in_vmem(blocks),
        in_hbm(inner_carry),
    )


def rest_kernel(
    order, table, window, blocks, inner, from_moments, near, maps, neighbours, rows, sems
):
    listed = pltpu.make_async_copy(table, neighbours, sems.at[0])
    fetch = pltpu.make_async_copy(from_moments, rows, sems.at[1])
    found = pltpu.make_async_copy(inner, near.at[pl.ds(len(order), inner.shape[0])], sems.at[2])
    for c in (listed, fetch, found):
        c.start()
    listed.wait()
    for i, cluster in enumerate(order):
        blocks_here = [blocks.at[lag, cluster] for lag in range(blocks.shape[0])]
        near[i], _ = near_of(neighbours, window, blocks_here, cluster)
    fetch.wait()
    w = jnp.transpose(rows[...], (1, 0, 2))
    for p in range(maps.shape[0]):
        x = jnp.concatenate([w[2 * p], w[2 * p + 1]], axis=1)
        maps[p] = jnp.concatenate([x, x], axis=0)
    found.wait()


def rest_near(neighbours, window, blocks, inner, from_moments, order):
    steps, unknowns = window.shape[1:]
    clusters = blocks.shape[1]
    terms = from_moments.shape[0]
    return pl.pallas_call(
        functools.partial(rest_kernel, order),
        in_specs=[HBM, VMEM, VMEM, HBM, HBM],
        out_specs=[VMEM] * 2,
        out_shape=[
            jax.ShapeDtypeStruct((len(order) + inner.shape[0], steps, unknowns), F32),
            jax.ShapeDtypeStruct((clusters // 2, 2 * terms, 2 * unknowns), BF16),
        ],
        scratch_shapes=[
            pltpu.SMEM(neighbours.shape, jnp.int32),
            pltpu.VMEM(from_moments.shape, BF16),
            pltpu.SemaphoreType.DMA((3,)),
        ],
        compiler_params=pltpu.CompilerParams(vmem_limit_bytes=8 << 20),
        name="rest",
    )(in_hbm(neighbours), window, in_vmem(blocks), in_hbm(inner), in_hbm(from_moments))


def final_kernel(places, edge, rest, carry, *refs):
    parts = refs[:4]
    maps, live, out, major, done, sems = refs[4:]
    steps, clusters, unknowns = out.shape
    terms = maps.shape[1] // 2
    first = lax.axis_index("space") * clusters
    total = parts[0][...].astype(F32)
    for part in parts[1:]:
        total = total + part[...].astype(F32)
    lane = lax.broadcasted_iota(jnp.int32, total.shape, 1)
    size = steps // 2
    chunk = 32
    row = lax.broadcasted_iota(jnp.int32, (8, unknowns), 0)
    copies = []
    for half in range(2):
        mine = jnp.where(lane // terms == half, total, 0.0).astype(BF16)
        here = pl.ds(half * size, size)
        alive = live[here, :]
        for p in range(clusters // 2):
            both = jnp.dot(mine, maps[p], preferred_element_type=F32)
            for q in range(2):
                c = 2 * p + q
                which, at = places[c]
                near = (edge, rest)[which]
                x = both[:, q * unknowns : (q + 1) * unknowns] + near[at, here, :]
                if half == 0:
                    head = jnp.where(row == 0, jnp.broadcast_to(carry[c], row.shape), 0.0)
                    x = jnp.concatenate([x[:8] + head, x[8:]], axis=0)
                major[c] = jnp.where(alive > first + c, x, 0.0).astype(BF16)
        for i in range(size // chunk):
            start = half * size + i * chunk
            rows = pl.ds(start, chunk)
            done[rows] = jnp.transpose(major[:, pl.ds(i * chunk, chunk), :], (1, 0, 2))
            copies.append(
                pltpu.make_async_copy(done.at[rows], out.at[rows], sems.at[start // chunk])
            )
            copies[-1].start()
    for copy in copies:
        copy.wait()


def final(edge, rest, carry, parts, maps, live, orders):
    steps, unknowns = live.shape
    clusters = carry.shape[0]
    places = {c: (k, i) for k, order in enumerate(orders) for i, c in enumerate(order)}
    return pl.pallas_call(
        functools.partial(final_kernel, places),
        in_specs=[VMEM] * (5 + len(parts)),
        out_specs=HBM,
        out_shape=jax.ShapeDtypeStruct((steps, clusters, unknowns), BF16),
        scratch_shapes=[
            pltpu.VMEM((clusters, steps // 2, unknowns), BF16),
            pltpu.VMEM((steps, clusters, unknowns), BF16),
            pltpu.SemaphoreType.DMA((steps // 32,)),
        ],
        compiler_params=pltpu.CompilerParams(vmem_limit_bytes=10 << 20),
        name="final",
    )(edge, rest, carry, *parts, maps, live)


def exchanged(x, axis):
    return lax.all_to_all(x, axis, split_axis=0, concat_axis=0, tiled=True)


def swapped_from(x, axis, start):
    count = lax.axis_size(axis)
    route = []
    for i in range(start, count - 1, 2):
        route += [(i, i + 1), (i + 1, i)]
    return lax.ppermute(x, axis, route)


def from_chip(x, axis, distance):
    count = lax.axis_size(axis)
    return lax.ppermute(x, axis, [(i, (i + 2 * distance) % count) for i in range(count)])


def passed_on(x, axis):
    count = lax.axis_size(axis)
    return lax.ppermute(x, axis, [(i, i + 1) for i in range(count - 1)])


def local(density, active, neighbours, near_blocks, to_moments, from_moments, decay_rates, lengths):
    steps = density.shape[0]
    slabs, chips = lax.axis_size("tm"), lax.axis_size("space") // 2
    window, pair, other, far, decay, ends, live = prep(
        density,
        active.reshape(1, steps),
        to_moments,
        decay_rates.reshape(1, -1),
        lengths.reshape(1, steps),
        slabs,
    )
    ends = exchanged(ends, "tm")
    from_pair = swapped_from(pair, "space", 0)
    from_other = swapped_from(other, "space", 1)
    neighbours = neighbours.T
    clusters = density.shape[1]
    quarter = REACH // 2
    middle = clusters // 2
    full = ((middle - 4, 2), (middle - 2, 2), (middle, 4))
    later = ((REACH, quarter), (clusters - REACH - quarter, quarter))
    low = tuple(range(REACH))
    high = tuple(range(clusters - REACH, clusters))
    inner, inner_carry = inner_near(neighbours, window, near_blocks, full, later)
    ends, inner, inner_carry = lax.optimization_barrier((ends, inner, inner_carry))
    mine = arrive(ends, far, decay)
    mine = pair_sum(mine, swapped_from(mine, "space", 0))
    parts = [mine] + [from_chip(mine, "space", d) for d in range(1, chips)]
    inner_carry, mine = lax.optimization_barrier((inner_carry, mine))
    edge, carry, window = edge_near(
        neighbours, window, from_pair, from_other, near_blocks, inner_carry, low, high
    )
    carry = passed_on(carry, "tm")
    others = clusters_of(later) + high
    rest, maps = rest_near(neighbours, window, near_blocks, inner, from_moments, others)
    return final(edge, rest, carry, parts, maps, live, (low, others + clusters_of(full)))


def solution(mesh):
    placed = (
        P("tm", "space", None),
        P("tm"),
        P("space", None),
        P(None, "space", None, None, None),
        P(None, "space", None),
        P(None, "space", None),
        P(),
        P("tm"),
    )
    return jax.shard_map(
        local, mesh=mesh, in_specs=placed, out_specs=P("tm", "space", None), check_vma=False
    )
```

```python
import functools

import jax
import jax.numpy as jnp
from jax import lax
from jax.experimental import pallas as pl
from jax.experimental.pallas import tpu as pltpu
from jax.sharding import PartitionSpec as P

REACH = 8
F32 = jnp.float32
BF16 = jnp.bfloat16
HBM = pl.BlockSpec(memory_space=pltpu.HBM)
VMEM = pl.BlockSpec(memory_space=pltpu.VMEM)


def in_hbm(x):
    return pltpu.with_memory_space_constraint(x, pltpu.HBM)


def in_vmem(x):
    return pltpu.with_memory_space_constraint(x, pltpu.VMEM)


def column(row, lanes):
    return jnp.transpose(jnp.broadcast_to(row, (lanes, row.shape[1])))


def shifted_down(v, steps, fill):
    rows = v.shape[0]
    if steps < 8:
        moved = pltpu.roll(v, steps, 0)
        at = lax.broadcasted_iota(jnp.int32, v.shape, 0)
        return jnp.where(at < steps, jnp.full_like(v, fill), moved)
    return jnp.concatenate([jnp.full((steps, v.shape[1]), fill, v.dtype), v[: rows - steps]], 0)


def doubled(row):
    return jnp.concatenate([row, row], axis=1)


def is_even():
    return lax.rem(lax.axis_index("space"), 2) == 0


def prep_kernel(
    density,
    active,
    to_moments,
    rates,
    lengths,
    window,
    pair,
    other,
    far,
    decay,
    ends,
    live,
    dense,
    maps,
    active_row,
    rates_row,
    lengths_row,
    flat,
    lines,
    sems,
):
    steps, clusters, unknowns = density.shape
    terms = to_moments.shape[0]
    pieces = 4
    size = steps // pieces
    chunk = 32
    pitch = clusters + 1
    first = lax.axis_index("space") * clusters

    def copy(src, dst, k):
        return pltpu.make_async_copy(src, dst, sems.at[k])

    small = [
        copy(active, active_row, 0),
        copy(lengths, lengths_row, 1),
        copy(rates, rates_row, 2),
    ]
    parts = [
        copy(density.at[pl.ds(k * size, size)], dense.at[pl.ds(k * size, size)], 4 + k)
        for k in range(pieces)
    ]
    weights = copy(to_moments, maps, 3)
    for c in small + parts + [weights]:
        c.start()
    for c in small:
        c.wait()
    live[...] = column(active_row[...], unknowns)

    for k in range(pieces):
        parts[k].wait()

        def spread(i, _):
            start = pl.multiple_of(k * size + i * chunk, chunk)
            here = pl.ds(start, chunk)
            x = dense[here].astype(F32)
            for t in range(chunk):
                flat[pl.ds(t * pitch, clusters), :] = x[t]
            alive = live[here, :]
            for c in range(clusters):
                y = flat[pl.ds(c, chunk, stride=pitch), :]
                y = jnp.where(alive > first + c, y, 0.0)
                window[REACH + c, here, :] = y.astype(BF16)
            return 0

        lax.fori_loop(0, size // chunk, spread, 0)

    even = is_even()
    above = clusters
    sides = [
        copy(window.at[pl.ds(jnp.where(even, above, REACH), REACH)], pair, 8),
        copy(window.at[pl.ds(jnp.where(even, REACH, above), REACH)], other, 9),
    ]
    for c in sides:
        c.start()

    weights.wait()
    w = jnp.transpose(maps[...], (1, 0, 2))
    total = jnp.zeros((steps, 2 * terms), F32)
    for c in range(0, clusters, 2):
        x = jnp.concatenate([window[REACH + c], window[REACH + c + 1]], axis=1)
        y = jnp.concatenate([w[c], w[c + 1]], axis=1)
        y = jnp.concatenate([y, y], axis=0)
        total = total + lax.dot_general(
            x, y, (((1,), (1,)), ((), ())), preferred_element_type=F32
        )
    d = jnp.exp(-doubled(rates_row[...]) * column(lengths_row[...], 2 * terms))
    s = 1
    while s < steps:
        before = shifted_down(total, s, 0.0)
        factor = shifted_down(d, s, 1.0)
        total = total + d * before
        d = d * factor
        s *= 2
    lane = lax.broadcasted_iota(jnp.int32, (1, 2 * terms), 1)
    line = jnp.where(lane < terms, total[steps - 1 :], d[steps - 1 :])
    for k in range(ends.shape[0]):
        lines[k] = line
    sides.append(copy(lines, ends, 10))
    sides[-1].start()
    scale = jnp.sqrt(2.0 * doubled(rates_row[...]))
    far[...] = shifted_down(total, 1, 0.0) * scale
    decay[...] = shifted_down(d, 1, 1.0) * scale
    for c in sides:
        c.wait()


def prep(density, active, to_moments, rates, lengths, slabs):
    steps, clusters, unknowns = density.shape
    terms = to_moments.shape[0]
    lanes = 2 * terms
    side = pltpu.HBM((REACH, steps, unknowns), BF16)
    return pl.pallas_call(
        prep_kernel,
        in_specs=[HBM] * 5,
        out_specs=[VMEM, HBM, HBM, VMEM, VMEM, HBM, VMEM],
        out_shape=[
            jax.ShapeDtypeStruct((clusters + 2 * REACH, steps, unknowns), BF16),
            side,
            side,
            jax.ShapeDtypeStruct((steps, lanes), F32),
            jax.ShapeDtypeStruct((steps, lanes), F32),
            pltpu.HBM((slabs, 1, lanes), F32),
            jax.ShapeDtypeStruct((steps, unknowns), jnp.int32),
        ],
        scratch_shapes=[
            pltpu.VMEM(density.shape, BF16),
            pltpu.VMEM(to_moments.shape, BF16),
            pltpu.VMEM(active.shape, jnp.int32),
            pltpu.VMEM(rates.shape, F32),
            pltpu.VMEM(lengths.shape, F32),
            pltpu.VMEM((32 * (clusters + 1) + 7, unknowns), F32),
            pltpu.VMEM((slabs, 1, lanes), F32),
            pltpu.SemaphoreType.DMA((11,)),
        ],
        compiler_params=pltpu.CompilerParams(vmem_limit_bytes=10 << 20),
        name="prep",
    )(*map(in_hbm, (density, active, to_moments, rates, lengths)))


def arrive_kernel(ends, far, decay, out):
    me = lax.axis_index("tm")
    slabs = ends.shape[0]
    steps, lanes = far.shape
    half = lanes // 2
    lane = lax.broadcasted_iota(jnp.int32, (1, lanes), 1)
    state = jnp.zeros((1, lanes), F32)
    for k in range(slabs):
        v = ends[k]
        swapped = pltpu.roll(v, half, 1)
        end = jnp.where(lane < half, v, swapped)
        factor = jnp.where(lane < half, swapped, v)
        state = jnp.where(k < me, factor * state + end, state)
    x = far[...] + decay[...] * state
    wide = lax.broadcasted_iota(jnp.int32, (steps // 2, lanes), 1)
    out[...] = jnp.where(wide < half, x[: steps // 2], x[steps // 2 :])


def arrive(ends, far, decay):
    steps, lanes = far.shape
    return pl.pallas_call(
        arrive_kernel,
        in_specs=[VMEM] * 3,
        out_specs=VMEM,
        out_shape=jax.ShapeDtypeStruct((steps // 2, lanes), F32),
        compiler_params=pltpu.CompilerParams(vmem_limit_bytes=4 << 20),
        cost_estimate=pl.CostEstimate(
            flops=10_000_000_000, bytes_accessed=1 << 20, transcendentals=0
        ),
        name="arrive",
    )(ends, far, decay)


def pair_kernel(a, b, out):
    out[...] = (a[...] + b[...]).astype(BF16)


def pair_sum(a, b):
    return pl.pallas_call(
        pair_kernel,
        in_specs=[VMEM] * 2,
        out_specs=VMEM,
        out_shape=jax.ShapeDtypeStruct(a.shape, BF16),
        compiler_params=pltpu.CompilerParams(vmem_limit_bytes=4 << 20),
        name="pair_sum",
    )(a, b)


def gathered(neighbours, window, cluster, rows):
    base = lax.axis_index("space") * neighbours.shape[1] - REACH
    return jnp.concatenate(
        [window[neighbours[j, cluster] - base, rows, :] for j in range(neighbours.shape[0])], axis=1
    )


def stacked(block):
    nb, unknowns, width = block.shape
    return block[...].reshape(nb * unknowns, width)


def near_of(neighbours, window, blocks, cluster):
    steps = window.shape[1]
    x = gathered(neighbours, window, cluster, pl.ds(0, steps))
    w = jnp.concatenate([stacked(block) for block in blocks], axis=1)
    both = jnp.dot(x, w, preferred_element_type=F32)
    now, later = jnp.split(both, 2, axis=1)
    return now + shifted_down(later, 1, 0.0), later[steps - 1 :]


def fetches_of(blocks, lags, groups, held, sems):
    waits, at = [], 0
    for k, (start, count) in enumerate(groups):
        waits.append(
            [
                pltpu.make_async_copy(
                    blocks.at[lag, pl.ds(start, count)],
                    held.at[n, pl.ds(at, count)],
                    sems.at[n, k],
                )
                for n, lag in enumerate(lags)
            ]
        )
        at += count
    return waits


def clusters_of(groups):
    return tuple(c for start, count in groups for c in range(start, start + count))


def near_groups(neighbours, window, groups, fetches, held, put):
    i = 0
    for (start, count), some in zip(groups, fetches):
        for fetch in some:
            fetch.wait()
        for cluster in range(start, start + count):
            blocks_here = [held.at[n, i] for n in range(held.shape[0])]
            put(i, cluster, *near_of(neighbours, window, blocks_here, cluster))
            i += 1


def inner_kernel(
    groups,
    later_groups,
    table,
    window,
    blocks,
    from_moments,
    near,
    carry,
    maps,
    neighbours,
    held,
    held_later,
    found,
    lines,
    rows,
    built,
    sems,
    later_sems,
    out_sems,
):
    lags = blocks.shape[0]
    listed = pltpu.make_async_copy(table, neighbours, out_sems.at[0])
    listed.start()
    fetches = fetches_of(blocks, range(lags), groups, held, sems)
    later_fetches = fetches_of(blocks, (lags - 1,), later_groups, held_later, later_sems)
    for some in fetches + later_fetches:
        for fetch in some:
            fetch.start()
    rows_fetch = pltpu.make_async_copy(from_moments, rows, out_sems.at[3])
    rows_fetch.start()
    listed.wait()

    def put(i, cluster, x, last):
        found[i] = x
        lines[cluster - REACH] = last

    near_groups(neighbours, window, groups, fetches, held, put)
    store = pltpu.make_async_copy(found, near, out_sems.at[1])
    store.start()
    i = 0
    for (start, count), some in zip(later_groups, later_fetches):
        for fetch in some:
            fetch.wait()
        for cluster in range(start, start + count):
            lines[cluster - REACH] = last_row(neighbours, window, held_later.at[0, i], cluster)
            i += 1
    lines_store = pltpu.make_async_copy(lines, carry, out_sems.at[2])
    lines_store.start()
    rows_fetch.wait()
    w = jnp.transpose(rows[...], (1, 0, 2))
    for p in range(maps.shape[0]):
        x = jnp.concatenate([w[2 * p], w[2 * p + 1]], axis=1)
        built[p] = jnp.concatenate([x, x], axis=0)
    maps_store = pltpu.make_async_copy(built, maps, out_sems.at[4])
    maps_store.start()
    store.wait()
    lines_store.wait()
    maps_store.wait()


def inner_near(neighbours, window, blocks, from_moments, groups, later_groups):
    steps, unknowns = window.shape[1:]
    lags, clusters, nb = blocks.shape[:3]
    count, more = len(clusters_of(groups)), len(clusters_of(later_groups))
    maps = (clusters // 2, 2 * from_moments.shape[0], 2 * unknowns)
    block = (nb, unknowns, unknowns)
    return pl.pallas_call(
        functools.partial(inner_kernel, groups, later_groups),
        in_specs=[HBM, VMEM, HBM, HBM],
        out_specs=[HBM] * 3,
        out_shape=[
            pltpu.HBM((count, steps, unknowns), F32),
            pltpu.HBM((count + more, 1, unknowns), F32),
            pltpu.HBM(maps, BF16),
        ],
        scratch_shapes=[
            pltpu.SMEM(neighbours.shape, jnp.int32),
            pltpu.VMEM((lags, count, *block), BF16),
            pltpu.VMEM((1, more, *block), BF16),
            pltpu.VMEM((count, steps, unknowns), F32),
            pltpu.VMEM((count + more, 1, unknowns), F32),
            pltpu.VMEM(from_moments.shape, BF16),
            pltpu.VMEM(maps, BF16),
            pltpu.SemaphoreType.DMA((lags, len(groups))),
            pltpu.SemaphoreType.DMA((1, len(later_groups))),
            pltpu.SemaphoreType.DMA((5,)),
        ],
        compiler_params=pltpu.CompilerParams(vmem_limit_bytes=18 << 20),
        name="inner",
    )(in_hbm(neighbours), window, in_hbm(blocks), in_hbm(from_moments))


def last_row(neighbours, window, block, cluster):
    steps = window.shape[1]
    x = gathered(neighbours, window, cluster, pl.ds(steps - 16, 16))
    return jnp.dot(x, stacked(block), preferred_element_type=F32)[15:]


def edge_kernel(
    early,
    order,
    ends_only,
    table,
    window_in,
    from_pair,
    from_other,
    blocks,
    inner_carry,
    near,
    carry,
    window,
    neighbours,
    sems,
):
    del window_in
    even = is_even()
    above = window.shape[0] - REACH
    lags = blocks.shape[0]

    def copy(src, dst, k):
        return pltpu.make_async_copy(src, dst, sems.at[k])

    sides = [
        copy(table, neighbours, 0),
        copy(from_pair, window.at[pl.ds(jnp.where(even, above, 0), REACH)], 1),
        copy(from_other, window.at[pl.ds(jnp.where(even, 0, above), REACH)], 2),
        copy(inner_carry, carry.at[pl.ds(REACH, inner_carry.shape[0])], 3),
    ]
    for c in sides:
        c.start()
    sides[0].wait()
    for i, cluster in enumerate(early):
        blocks_here = [blocks.at[lag, cluster] for lag in range(lags)]
        near[i], _ = near_of(neighbours, window, blocks_here, cluster)
    for c in sides[1:]:
        c.wait()
    for i, cluster in enumerate(order, len(early)):
        blocks_here = [blocks.at[lag, cluster] for lag in range(lags)]
        near[i], carry[cluster] = near_of(neighbours, window, blocks_here, cluster)
    for cluster in ends_only:
        carry[cluster] = last_row(neighbours, window, blocks.at[lags - 1, cluster], cluster)


def edge_near(
    neighbours, window, from_pair, from_other, blocks, inner_carry, early, order, ends_only
):
    steps, unknowns = window.shape[1:]
    clusters = blocks.shape[1]
    return pl.pallas_call(
        functools.partial(edge_kernel, early, order, ends_only),
        in_specs=[HBM, VMEM, HBM, HBM, VMEM, HBM],
        out_specs=[VMEM] * 3,
        out_shape=[
            jax.ShapeDtypeStruct((len(early) + len(order), steps, unknowns), F32),
            jax.ShapeDtypeStruct((clusters, 1, unknowns), F32),
            jax.ShapeDtypeStruct(window.shape, BF16),
        ],
        scratch_shapes=[
            pltpu.SMEM(neighbours.shape, jnp.int32),
            pltpu.SemaphoreType.DMA((4,)),
        ],
        input_output_aliases={1: 2},
        compiler_params=pltpu.CompilerParams(vmem_limit_bytes=8 << 20),
        name="edge",
    )(
        in_hbm(neighbours),
        window,
        in_hbm(from_pair),
        in_hbm(from_other),
        in_vmem(blocks),
        in_hbm(inner_carry),
    )


def rest_kernel(order, table, window, blocks, inner, found_maps, near, maps, neighbours, sems):
    listed = pltpu.make_async_copy(table, neighbours, sems.at[0])
    fetches = [
        pltpu.make_async_copy(found_maps, maps, sems.at[1]),
        pltpu.make_async_copy(inner, near.at[pl.ds(len(order), inner.shape[0])], sems.at[2]),
    ]
    listed.start()
    for fetch in fetches:
        fetch.start()
    listed.wait()
    for i, cluster in enumerate(order):
        blocks_here = [blocks.at[lag, cluster] for lag in range(blocks.shape[0])]
        near[i], _ = near_of(neighbours, window, blocks_here, cluster)
    for fetch in fetches:
        fetch.wait()


def rest_near(neighbours, window, blocks, inner, maps, order):
    steps, unknowns = window.shape[1:]
    return pl.pallas_call(
        functools.partial(rest_kernel, order),
        in_specs=[HBM, VMEM, VMEM, HBM, HBM],
        out_specs=[VMEM] * 2,
        out_shape=[
            jax.ShapeDtypeStruct((len(order) + inner.shape[0], steps, unknowns), F32),
            jax.ShapeDtypeStruct(maps.shape, BF16),
        ],
        scratch_shapes=[
            pltpu.SMEM(neighbours.shape, jnp.int32),
            pltpu.SemaphoreType.DMA((3,)),
        ],
        compiler_params=pltpu.CompilerParams(vmem_limit_bytes=8 << 20),
        name="rest",
    )(in_hbm(neighbours), window, in_vmem(blocks), in_hbm(inner), in_hbm(maps))


def final_kernel(places, edge, rest, carry, *refs):
    parts = refs[:4]
    maps, live, out, major, done, sems = refs[4:]
    steps, clusters, unknowns = out.shape
    terms = maps.shape[1] // 2
    first = lax.axis_index("space") * clusters
    total = parts[0][...].astype(F32)
    for part in parts[1:]:
        total = total + part[...].astype(F32)
    lane = lax.broadcasted_iota(jnp.int32, total.shape, 1)
    size = steps // 2
    chunk = 32
    row = lax.broadcasted_iota(jnp.int32, (8, unknowns), 0)
    copies = []
    for half in range(2):
        mine = jnp.where(lane // terms == half, total, 0.0).astype(BF16)
        here = pl.ds(half * size, size)
        alive = live[here, :]
        for p in range(clusters // 2):
            both = jnp.dot(mine, maps[p], preferred_element_type=F32)
            for q in range(2):
                c = 2 * p + q
                which, at = places[c]
                near = (edge, rest)[which]
                x = both[:, q * unknowns : (q + 1) * unknowns] + near[at, here, :]
                if half == 0:
                    head = jnp.where(row == 0, jnp.broadcast_to(carry[c], row.shape), 0.0)
                    x = jnp.concatenate([x[:8] + head, x[8:]], axis=0)
                major[c] = jnp.where(alive > first + c, x, 0.0).astype(BF16)
        for i in range(size // chunk):
            start = half * size + i * chunk
            rows = pl.ds(start, chunk)
            done[rows] = jnp.transpose(major[:, pl.ds(i * chunk, chunk), :], (1, 0, 2))
            copies.append(
                pltpu.make_async_copy(done.at[rows], out.at[rows], sems.at[start // chunk])
            )
            copies[-1].start()
    for copy in copies:
        copy.wait()


def final(edge, rest, carry, parts, maps, live, orders):
    steps, unknowns = live.shape
    clusters = carry.shape[0]
    places = {c: (k, i) for k, order in enumerate(orders) for i, c in enumerate(order)}
    return pl.pallas_call(
        functools.partial(final_kernel, places),
        in_specs=[VMEM] * (5 + len(parts)),
        out_specs=HBM,
        out_shape=jax.ShapeDtypeStruct((steps, clusters, unknowns), BF16),
        scratch_shapes=[
            pltpu.VMEM((clusters, steps // 2, unknowns), BF16),
            pltpu.VMEM((steps, clusters, unknowns), BF16),
            pltpu.SemaphoreType.DMA((steps // 32,)),
        ],
        compiler_params=pltpu.CompilerParams(vmem_limit_bytes=10 << 20),
        name="final",
    )(edge, rest, carry, *parts, maps, live)


def exchanged(x, axis):
    return lax.all_to_all(x, axis, split_axis=0, concat_axis=0, tiled=True)


def swapped_from(x, axis, start):
    count = lax.axis_size(axis)
    route = []
    for i in range(start, count - 1, 2):
        route += [(i, i + 1), (i + 1, i)]
    return lax.ppermute(x, axis, route)


def from_chip(x, axis, distance):
    count = lax.axis_size(axis)
    return lax.ppermute(x, axis, [(i, (i + 2 * distance) % count) for i in range(count)])


def passed_on(x, axis):
    count = lax.axis_size(axis)
    return lax.ppermute(x, axis, [(i, i + 1) for i in range(count - 1)])


def local(density, active, neighbours, near_blocks, to_moments, from_moments, decay_rates, lengths):
    steps = density.shape[0]
    slabs, chips = lax.axis_size("tm"), lax.axis_size("space") // 2
    window, pair, other, far, decay, ends, live = prep(
        density,
        active.reshape(1, steps),
        to_moments,
        decay_rates.reshape(1, -1),
        lengths.reshape(1, steps),
        slabs,
    )
    ends = exchanged(ends, "tm")
    from_pair = swapped_from(pair, "space", 0)
    from_other = swapped_from(other, "space", 1)
    neighbours = neighbours.T
    clusters = density.shape[1]
    quarter = REACH // 2
    middle = clusters // 2
    full = ((middle - 4, 2), (middle - 2, 2), (middle, 4))
    later = ((REACH, quarter), (clusters - REACH - quarter, quarter))
    low = tuple(range(REACH))
    high = tuple(range(clusters - REACH, clusters))
    inner, inner_carry, maps = inner_near(
        neighbours, window, near_blocks, from_moments, full, later
    )
    ends, inner, inner_carry = lax.optimization_barrier((ends, inner, inner_carry))
    mine = arrive(ends, far, decay)
    mine = pair_sum(mine, swapped_from(mine, "space", 0))
    parts = [mine] + [from_chip(mine, "space", d) for d in range(1, chips)]
    inner_carry, mine = lax.optimization_barrier((inner_carry, mine))
    later = clusters_of(later)
    early, others = later[:3], later[3:] + high
    edge, carry, window = edge_near(
        neighbours, window, from_pair, from_other, near_blocks, inner_carry, early, low, high
    )
    carry = passed_on(carry, "tm")
    rest, maps = rest_near(neighbours, window, near_blocks, inner, maps, others)
    return final(edge, rest, carry, parts, maps, live, (early + low, others + clusters_of(full)))


def solution(mesh):
    placed = (
        P("tm", "space", None),
        P("tm"),
        P("space", None),
        P(None, "space", None, None, None),
        P(None, "space", None),
        P(None, "space", None),
        P(),
        P("tm"),
    )
    return jax.shard_map(
        local, mesh=mesh, in_specs=placed, out_specs=P("tm", "space", None), check_vma=False
    )
```

```python
import functools

import jax
import jax.numpy as jnp
from jax import lax
from jax.experimental import pallas as pl
from jax.experimental.pallas import tpu as pltpu
from jax.sharding import PartitionSpec as P

REACH = 8
F32 = jnp.float32
BF16 = jnp.bfloat16
HBM = pl.BlockSpec(memory_space=pltpu.HBM)
VMEM = pl.BlockSpec(memory_space=pltpu.VMEM)


def in_hbm(x):
    return pltpu.with_memory_space_constraint(x, pltpu.HBM)


def in_vmem(x):
    return pltpu.with_memory_space_constraint(x, pltpu.VMEM)


def column(row, lanes):
    return jnp.transpose(jnp.broadcast_to(row, (lanes, row.shape[1])))


def shifted_down(v, steps, fill):
    rows = v.shape[0]
    if steps < 8:
        moved = pltpu.roll(v, steps, 0)
        at = lax.broadcasted_iota(jnp.int32, v.shape, 0)
        return jnp.where(at < steps, jnp.full_like(v, fill), moved)
    return jnp.concatenate([jnp.full((steps, v.shape[1]), fill, v.dtype), v[: rows - steps]], 0)


def doubled(row):
    return jnp.concatenate([row, row], axis=1)


def is_even():
    return lax.rem(lax.axis_index("space"), 2) == 0


def prep_kernel(
    density,
    active,
    to_moments,
    rates,
    lengths,
    window,
    pair,
    other,
    far,
    decay,
    ends,
    live,
    dense,
    maps,
    active_row,
    rates_row,
    lengths_row,
    flat,
    lines,
    sems,
):
    steps, clusters, unknowns = density.shape
    terms = to_moments.shape[0]
    pieces = 4
    size = steps // pieces
    chunk = 32
    pitch = clusters + 1
    first = lax.axis_index("space") * clusters

    def copy(src, dst, k):
        return pltpu.make_async_copy(src, dst, sems.at[k])

    small = [
        copy(active, active_row, 0),
        copy(lengths, lengths_row, 1),
        copy(rates, rates_row, 2),
    ]
    parts = [
        copy(density.at[pl.ds(k * size, size)], dense.at[pl.ds(k * size, size)], 4 + k)
        for k in range(pieces)
    ]
    weights = copy(to_moments, maps, 3)
    for c in small + parts + [weights]:
        c.start()
    for c in small:
        c.wait()
    live[...] = column(active_row[...], unknowns)

    for k in range(pieces):
        parts[k].wait()

        def spread(i, _):
            start = pl.multiple_of(k * size + i * chunk, chunk)
            here = pl.ds(start, chunk)
            x = dense[here].astype(F32)
            for t in range(chunk):
                flat[pl.ds(t * pitch, clusters), :] = x[t]
            alive = live[here, :]
            for c in range(clusters):
                y = flat[pl.ds(c, chunk, stride=pitch), :]
                y = jnp.where(alive > first + c, y, 0.0)
                window[REACH + c, here, :] = y.astype(BF16)
            return 0

        lax.fori_loop(0, size // chunk, spread, 0)

    even = is_even()
    above = clusters
    sides = [
        copy(window.at[pl.ds(jnp.where(even, above, REACH), REACH)], pair, 8),
        copy(window.at[pl.ds(jnp.where(even, REACH, above), REACH)], other, 9),
    ]
    for c in sides:
        c.start()

    weights.wait()
    w = jnp.transpose(maps[...], (1, 0, 2))
    total = jnp.zeros((steps, 2 * terms), F32)
    for c in range(0, clusters, 2):
        x = jnp.concatenate([window[REACH + c], window[REACH + c + 1]], axis=1)
        y = jnp.concatenate([w[c], w[c + 1]], axis=1)
        y = jnp.concatenate([y, y], axis=0)
        total = total + lax.dot_general(
            x, y, (((1,), (1,)), ((), ())), preferred_element_type=F32
        )
    d = jnp.exp(-doubled(rates_row[...]) * column(lengths_row[...], 2 * terms))
    s = 1
    while s < steps:
        before = shifted_down(total, s, 0.0)
        factor = shifted_down(d, s, 1.0)
        total = total + d * before
        d = d * factor
        s *= 2
    lane = lax.broadcasted_iota(jnp.int32, (1, 2 * terms), 1)
    line = jnp.where(lane < terms, total[steps - 1 :], d[steps - 1 :])
    for k in range(ends.shape[0]):
        lines[k] = line
    sides.append(copy(lines, ends, 10))
    sides[-1].start()
    scale = jnp.sqrt(2.0 * doubled(rates_row[...]))
    far[...] = shifted_down(total, 1, 0.0) * scale
    decay[...] = shifted_down(d, 1, 1.0) * scale
    for c in sides:
        c.wait()


def prep(density, active, to_moments, rates, lengths, slabs):
    steps, clusters, unknowns = density.shape
    terms = to_moments.shape[0]
    lanes = 2 * terms
    side = pltpu.HBM((REACH, steps, unknowns), BF16)
    return pl.pallas_call(
        prep_kernel,
        in_specs=[HBM] * 5,
        out_specs=[VMEM, HBM, HBM, VMEM, VMEM, HBM, VMEM],
        out_shape=[
            jax.ShapeDtypeStruct((clusters + 2 * REACH, steps, unknowns), BF16),
            side,
            side,
            jax.ShapeDtypeStruct((steps, lanes), F32),
            jax.ShapeDtypeStruct((steps, lanes), F32),
            pltpu.HBM((slabs, 1, lanes), F32),
            jax.ShapeDtypeStruct((steps, unknowns), jnp.int32),
        ],
        scratch_shapes=[
            pltpu.VMEM(density.shape, BF16),
            pltpu.VMEM(to_moments.shape, BF16),
            pltpu.VMEM(active.shape, jnp.int32),
            pltpu.VMEM(rates.shape, F32),
            pltpu.VMEM(lengths.shape, F32),
            pltpu.VMEM((32 * (clusters + 1) + 7, unknowns), F32),
            pltpu.VMEM((slabs, 1, lanes), F32),
            pltpu.SemaphoreType.DMA((11,)),
        ],
        compiler_params=pltpu.CompilerParams(vmem_limit_bytes=10 << 20),
        name="prep",
    )(*map(in_hbm, (density, active, to_moments, rates, lengths)))


def arrive_kernel(ends, far, decay, out):
    me = lax.axis_index("tm")
    slabs = ends.shape[0]
    steps, lanes = far.shape
    half = lanes // 2
    lane = lax.broadcasted_iota(jnp.int32, (1, lanes), 1)
    state = jnp.zeros((1, lanes), F32)
    for k in range(slabs):
        v = ends[k]
        swapped = pltpu.roll(v, half, 1)
        end = jnp.where(lane < half, v, swapped)
        factor = jnp.where(lane < half, swapped, v)
        state = jnp.where(k < me, factor * state + end, state)
    x = far[...] + decay[...] * state
    wide = lax.broadcasted_iota(jnp.int32, (steps // 2, lanes), 1)
    out[...] = jnp.where(wide < half, x[: steps // 2], x[steps // 2 :])


def arrive(ends, far, decay):
    steps, lanes = far.shape
    return pl.pallas_call(
        arrive_kernel,
        in_specs=[VMEM] * 3,
        out_specs=VMEM,
        out_shape=jax.ShapeDtypeStruct((steps // 2, lanes), F32),
        compiler_params=pltpu.CompilerParams(vmem_limit_bytes=4 << 20),
        cost_estimate=pl.CostEstimate(
            flops=10_000_000_000, bytes_accessed=1 << 20, transcendentals=0
        ),
        name="arrive",
    )(ends, far, decay)


def pair_kernel(a, b, out):
    out[...] = (a[...] + b[...]).astype(BF16)


def pair_sum(a, b):
    return pl.pallas_call(
        pair_kernel,
        in_specs=[VMEM] * 2,
        out_specs=VMEM,
        out_shape=jax.ShapeDtypeStruct(a.shape, BF16),
        compiler_params=pltpu.CompilerParams(vmem_limit_bytes=4 << 20),
        name="pair_sum",
    )(a, b)


def gathered(neighbours, window, cluster, rows):
    base = lax.axis_index("space") * neighbours.shape[1] - REACH
    return jnp.concatenate(
        [window[neighbours[j, cluster] - base, rows, :] for j in range(neighbours.shape[0])], axis=1
    )


def stacked(block):
    nb, unknowns, width = block.shape
    return block[...].reshape(nb * unknowns, width)


def near_of(neighbours, window, blocks, cluster):
    steps = window.shape[1]
    x = gathered(neighbours, window, cluster, pl.ds(0, steps))
    w = jnp.concatenate([stacked(block) for block in blocks], axis=1)
    both = jnp.dot(x, w, preferred_element_type=F32)
    now, later = jnp.split(both, 2, axis=1)
    return now + shifted_down(later, 1, 0.0), later[steps - 1 :]


def fetches_of(blocks, lags, groups, held, sems):
    waits, at = [], 0
    for k, (start, count) in enumerate(groups):
        waits.append(
            [
                pltpu.make_async_copy(
                    blocks.at[lag, pl.ds(start, count)],
                    held.at[n, pl.ds(at, count)],
                    sems.at[n, k],
                )
                for n, lag in enumerate(lags)
            ]
        )
        at += count
    return waits


def clusters_of(groups):
    return tuple(c for start, count in groups for c in range(start, start + count))


def near_groups(neighbours, window, groups, fetches, held, put):
    i = 0
    for (start, count), some in zip(groups, fetches):
        for fetch in some:
            fetch.wait()
        for cluster in range(start, start + count):
            blocks_here = [held.at[n, i] for n in range(held.shape[0])]
            put(i, cluster, *near_of(neighbours, window, blocks_here, cluster))
            i += 1


def inner_kernel(
    groups,
    later_groups,
    table,
    window,
    blocks,
    from_moments,
    near,
    carry,
    maps,
    neighbours,
    held,
    held_later,
    found,
    lines,
    rows,
    built,
    sems,
    later_sems,
    out_sems,
):
    lags = blocks.shape[0]
    listed = pltpu.make_async_copy(table, neighbours, out_sems.at[0])
    listed.start()
    fetches = fetches_of(blocks, range(lags), groups, held, sems)
    later_fetches = fetches_of(blocks, (lags - 1,), later_groups, held_later, later_sems)
    for some in fetches + later_fetches:
        for fetch in some:
            fetch.start()
    rows_fetch = pltpu.make_async_copy(from_moments, rows, out_sems.at[3])
    rows_fetch.start()
    listed.wait()

    def put(i, cluster, x, last):
        found[i] = x
        lines[cluster - REACH] = last

    near_groups(neighbours, window, groups, fetches, held, put)
    store = pltpu.make_async_copy(found, near, out_sems.at[1])
    store.start()
    i = 0
    for (start, count), some in zip(later_groups, later_fetches):
        for fetch in some:
            fetch.wait()
        for cluster in range(start, start + count):
            lines[cluster - REACH] = last_row(neighbours, window, held_later.at[0, i], cluster)
            i += 1
    lines_store = pltpu.make_async_copy(lines, carry, out_sems.at[2])
    lines_store.start()
    rows_fetch.wait()
    w = jnp.transpose(rows[...], (1, 0, 2))
    for p in range(maps.shape[0]):
        x = jnp.concatenate([w[2 * p], w[2 * p + 1]], axis=1)
        built[p] = jnp.concatenate([x, x], axis=0)
    maps_store = pltpu.make_async_copy(built, maps, out_sems.at[4])
    maps_store.start()
    store.wait()
    lines_store.wait()
    maps_store.wait()


def inner_near(neighbours, window, blocks, from_moments, groups, later_groups):
    steps, unknowns = window.shape[1:]
    lags, clusters, nb = blocks.shape[:3]
    count, more = len(clusters_of(groups)), len(clusters_of(later_groups))
    maps = (clusters // 2, 2 * from_moments.shape[0], 2 * unknowns)
    block = (nb, unknowns, unknowns)
    return pl.pallas_call(
        functools.partial(inner_kernel, groups, later_groups),
        in_specs=[HBM, VMEM, HBM, HBM],
        out_specs=[HBM] * 3,
        out_shape=[
            pltpu.HBM((count, steps, unknowns), F32),
            pltpu.HBM((count + more, 1, unknowns), F32),
            pltpu.HBM(maps, BF16),
        ],
        scratch_shapes=[
            pltpu.SMEM(neighbours.shape, jnp.int32),
            pltpu.VMEM((lags, count, *block), BF16),
            pltpu.VMEM((1, more, *block), BF16),
            pltpu.VMEM((count, steps, unknowns), F32),
            pltpu.VMEM((count + more, 1, unknowns), F32),
            pltpu.VMEM(from_moments.shape, BF16),
            pltpu.VMEM(maps, BF16),
            pltpu.SemaphoreType.DMA((lags, len(groups))),
            pltpu.SemaphoreType.DMA((1, len(later_groups))),
            pltpu.SemaphoreType.DMA((5,)),
        ],
        compiler_params=pltpu.CompilerParams(vmem_limit_bytes=18 << 20),
        name="inner",
    )(in_hbm(neighbours), window, in_hbm(blocks), in_hbm(from_moments))


def last_row(neighbours, window, block, cluster):
    steps = window.shape[1]
    x = gathered(neighbours, window, cluster, pl.ds(steps - 16, 16))
    return jnp.dot(x, stacked(block), preferred_element_type=F32)[15:]


def edge_kernel(
    early,
    order,
    ends_only,
    table,
    window_in,
    from_pair,
    from_other,
    blocks,
    inner_carry,
    near,
    carry,
    window,
    neighbours,
    sems,
):
    del window_in
    even = is_even()
    above = window.shape[0] - REACH
    lags = blocks.shape[0]

    def copy(src, dst, k):
        return pltpu.make_async_copy(src, dst, sems.at[k])

    sides = [
        copy(table, neighbours, 0),
        copy(from_pair, window.at[pl.ds(jnp.where(even, above, 0), REACH)], 1),
        copy(from_other, window.at[pl.ds(jnp.where(even, 0, above), REACH)], 2),
        copy(inner_carry, carry.at[pl.ds(REACH, inner_carry.shape[0])], 3),
    ]
    for c in sides:
        c.start()
    sides[0].wait()
    for i, cluster in enumerate(early):
        blocks_here = [blocks.at[lag, cluster] for lag in range(lags)]
        near[i], _ = near_of(neighbours, window, blocks_here, cluster)
    for c in sides[1:]:
        c.wait()
    for i, cluster in enumerate(order, len(early)):
        blocks_here = [blocks.at[lag, cluster] for lag in range(lags)]
        near[i], carry[cluster] = near_of(neighbours, window, blocks_here, cluster)
    for cluster in ends_only:
        carry[cluster] = last_row(neighbours, window, blocks.at[lags - 1, cluster], cluster)


def edge_near(
    neighbours, window, from_pair, from_other, blocks, inner_carry, early, order, ends_only
):
    steps, unknowns = window.shape[1:]
    clusters = blocks.shape[1]
    return pl.pallas_call(
        functools.partial(edge_kernel, early, order, ends_only),
        in_specs=[HBM, VMEM, HBM, HBM, VMEM, HBM],
        out_specs=[VMEM] * 3,
        out_shape=[
            jax.ShapeDtypeStruct((len(early) + len(order), steps, unknowns), F32),
            jax.ShapeDtypeStruct((clusters, 1, unknowns), F32),
            jax.ShapeDtypeStruct(window.shape, BF16),
        ],
        scratch_shapes=[
            pltpu.SMEM(neighbours.shape, jnp.int32),
            pltpu.SemaphoreType.DMA((4,)),
        ],
        input_output_aliases={1: 2},
        compiler_params=pltpu.CompilerParams(vmem_limit_bytes=8 << 20),
        name="edge",
    )(
        in_hbm(neighbours),
        window,
        in_hbm(from_pair),
        in_hbm(from_other),
        in_vmem(blocks),
        in_hbm(inner_carry),
    )


def rest_kernel(order, table, window, blocks, inner, found_maps, near, maps, neighbours, sems):
    listed = pltpu.make_async_copy(table, neighbours, sems.at[0])
    fetches = [
        pltpu.make_async_copy(found_maps, maps, sems.at[1]),
        pltpu.make_async_copy(inner, near.at[pl.ds(len(order), inner.shape[0])], sems.at[2]),
    ]
    listed.start()
    for fetch in fetches:
        fetch.start()
    listed.wait()
    for i, cluster in enumerate(order):
        blocks_here = [blocks.at[lag, cluster] for lag in range(blocks.shape[0])]
        near[i], _ = near_of(neighbours, window, blocks_here, cluster)
    for fetch in fetches:
        fetch.wait()


def rest_near(neighbours, window, blocks, inner, maps, order):
    steps, unknowns = window.shape[1:]
    return pl.pallas_call(
        functools.partial(rest_kernel, order),
        in_specs=[HBM, VMEM, VMEM, HBM, HBM],
        out_specs=[VMEM] * 2,
        out_shape=[
            jax.ShapeDtypeStruct((len(order) + inner.shape[0], steps, unknowns), F32),
            jax.ShapeDtypeStruct(maps.shape, BF16),
        ],
        scratch_shapes=[
            pltpu.SMEM(neighbours.shape, jnp.int32),
            pltpu.SemaphoreType.DMA((3,)),
        ],
        compiler_params=pltpu.CompilerParams(vmem_limit_bytes=8 << 20),
        name="rest",
    )(in_hbm(neighbours), window, in_vmem(blocks), in_hbm(inner), in_hbm(maps))


def final_kernel(places, edge, rest, carry, *refs):
    parts = refs[:4]
    maps, live, out, major, done, sems = refs[4:]
    steps, clusters, unknowns = out.shape
    terms = maps.shape[1] // 2
    first = lax.axis_index("space") * clusters
    total = parts[0][...].astype(F32)
    for part in parts[1:]:
        total = total + part[...].astype(F32)
    lane = lax.broadcasted_iota(jnp.int32, total.shape, 1)
    size = steps // 2
    chunk = 32
    row = lax.broadcasted_iota(jnp.int32, (8, unknowns), 0)
    copies = []
    for half in range(2):
        mine = jnp.where(lane // terms == half, total, 0.0).astype(BF16)
        here = pl.ds(half * size, size)
        alive = live[here, :]
        for p in range(clusters // 2):
            both = jnp.dot(mine, maps[p], preferred_element_type=F32)
            for q in range(2):
                c = 2 * p + q
                which, at = places[c]
                near = (edge, rest)[which]
                x = both[:, q * unknowns : (q + 1) * unknowns] + near[at, here, :]
                if half == 0:
                    head = jnp.where(row == 0, jnp.broadcast_to(carry[c], row.shape), 0.0)
                    x = jnp.concatenate([x[:8] + head, x[8:]], axis=0)
                major[c] = jnp.where(alive > first + c, x, 0.0).astype(BF16)
        for i in range(size // chunk):
            start = half * size + i * chunk
            rows = pl.ds(start, chunk)
            done[rows] = jnp.transpose(major[:, pl.ds(i * chunk, chunk), :], (1, 0, 2))
            copies.append(
                pltpu.make_async_copy(done.at[rows], out.at[rows], sems.at[start // chunk])
            )
            copies[-1].start()
    for copy in copies:
        copy.wait()


def final(edge, rest, carry, parts, maps, live, orders):
    steps, unknowns = live.shape
    clusters = carry.shape[0]
    places = {c: (k, i) for k, order in enumerate(orders) for i, c in enumerate(order)}
    return pl.pallas_call(
        functools.partial(final_kernel, places),
        in_specs=[VMEM] * (5 + len(parts)),
        out_specs=HBM,
        out_shape=jax.ShapeDtypeStruct((steps, clusters, unknowns), BF16),
        scratch_shapes=[
            pltpu.VMEM((clusters, steps // 2, unknowns), BF16),
            pltpu.VMEM((steps, clusters, unknowns), BF16),
            pltpu.SemaphoreType.DMA((steps // 32,)),
        ],
        compiler_params=pltpu.CompilerParams(vmem_limit_bytes=10 << 20),
        name="final",
    )(edge, rest, carry, *parts, maps, live)


def exchanged(x, axis):
    return lax.all_to_all(x, axis, split_axis=0, concat_axis=0, tiled=True)


def swapped_from(x, axis, start):
    count = lax.axis_size(axis)
    route = []
    for i in range(start, count - 1, 2):
        route += [(i, i + 1), (i + 1, i)]
    return lax.ppermute(x, axis, route)


def from_chip(x, axis, distance):
    count = lax.axis_size(axis)
    return lax.ppermute(x, axis, [(i, (i + 2 * distance) % count) for i in range(count)])


def passed_on(x, axis):
    count = lax.axis_size(axis)
    return lax.ppermute(x, axis, [(i, i + 1) for i in range(count - 1)])


def local(density, active, neighbours, near_blocks, to_moments, from_moments, decay_rates, lengths):
    steps = density.shape[0]
    slabs, chips = lax.axis_size("tm"), lax.axis_size("space") // 2
    window, pair, other, far, decay, ends, live = prep(
        density,
        active.reshape(1, steps),
        to_moments,
        decay_rates.reshape(1, -1),
        lengths.reshape(1, steps),
        slabs,
    )
    ends = exchanged(ends, "tm")
    from_pair = swapped_from(pair, "space", 0)
    from_other = swapped_from(other, "space", 1)
    neighbours = neighbours.T
    clusters = density.shape[1]
    quarter = REACH // 2
    middle = clusters // 2
    full = ((middle - 4, 2), (middle - 2, 2), (middle, 4))
    later = ((REACH, quarter), (clusters - REACH - quarter, quarter))
    low = tuple(range(REACH))
    high = tuple(range(clusters - REACH, clusters))
    inner, inner_carry, maps = inner_near(
        neighbours, window, near_blocks, from_moments, full, later
    )
    ends, inner, inner_carry = lax.optimization_barrier((ends, inner, inner_carry))
    mine = arrive(ends, far, decay)
    mine = pair_sum(mine, swapped_from(mine, "space", 0))
    parts = [mine] + [from_chip(mine, "space", d) for d in range(1, chips)]
    inner_carry, mine = lax.optimization_barrier((inner_carry, mine))
    later = clusters_of(later)
    early, others = (), later + high
    edge, carry, window = edge_near(
        neighbours, window, from_pair, from_other, near_blocks, inner_carry, early, low, high
    )
    carry = passed_on(carry, "tm")
    rest, maps = rest_near(neighbours, window, near_blocks, inner, maps, others)
    return final(edge, rest, carry, parts, maps, live, (early + low, others + clusters_of(full)))


def solution(mesh):
    placed = (
        P("tm", "space", None),
        P("tm"),
        P("space", None),
        P(None, "space", None, None, None),
        P(None, "space", None),
        P(None, "space", None),
        P(),
        P("tm"),
    )
    return jax.shard_map(
        local, mesh=mesh, in_specs=placed, out_specs=P("tm", "space", None), check_vma=False
    )
```
